768 devices in a mesh: energy: 24 (over y_lo, z), tile: 32 (over y_hi, x, core).
Axes of the slice: x: 4, y: 8 (y_hi: 4, y_lo: 2; y = y_hi * 2 + y_lo), z: 12, core: 2. Of those that a mesh axis runs over, the one named last changes fastest.
Arguments:
- g_less: bfloat16 [2, 768, 16384], P(None, 'energy', 'tile'), may hold values from -6 to 6
- g_great: bfloat16 [2, 768, 16384], P(None, 'energy', 'tile'), may hold values from -6 to 6
- coulomb: float32 [16384], P('tile'), may hold values from 0.3 to 3
- precond: bfloat16 [3, 16384, 512], P(None, 'tile'), may hold values from -0.25 to 0.25
Outputs:
- polar: float32 [768, 16384], P('energy', 'tile')
- screened: float32 [768, 16384], P('energy', 'tile')
The draws below stay inside these ranges and needn't reach their ends.
All inputs are finite; a program needn't handle non-finite values.
Results may differ from the reference program's by a relative error of at most 0.008.
Values may be sent and summed in bfloat16 or wider, within the bound.
No kernel may reach another device: no remote copies, remote signals or barrier semaphores. Data moves between devices by JAX's collectives and lax.ppermute only.
A program may use at most 32 MiB of HBM per device.

```python
import math
import jax
import jax.numpy as jnp

TILE_ORDER = 512
ITERS = 2
NE = 768
NORB = 16384
N_TILE = 32


def block_scale(own_key, extent, pieces, smallest, high):
    gain = 1.0
    for axis_at, parts in pieces:
        steps = jax.random.uniform(jax.random.fold_in(jax.random.fold_in(own_key, 6), axis_at), (parts,), jnp.float32, smallest / len(pieces), high / len(pieces))
        gain = gain * jnp.repeat(jnp.exp(steps), extent[axis_at] // parts).reshape((-1,) + (1,) * (len(extent) - 1 - axis_at))
    return gain


def centred(key, dims, deviation, bound, shards=(), held_as=jnp.bfloat16):
    loudness = block_scale(key, dims, shards, -0.22, 0.18) if shards else 1.0
    array = jax.random.normal(key, dims, jnp.float32) * deviation * loudness
    return jnp.minimum(jnp.maximum(array, -bound), bound).astype(held_as)


def setup_inputs(seed: int = 0) -> dict:
    splits = jax.random.split(jax.random.key(seed), 5)
    g_less = centred(splits[0], (2, NE, NORB), 1.0, 6.0, ((1, 24), (2, 32)))
    g_great = centred(splits[1], (2, NE, NORB), 1.0, 6.0, ((1, 24), (2, 32)))
    coulomb = jnp.clip(jnp.exp(math.log(3.0) - 2.3025851 * jax.random.uniform(splits[2], (NORB,), jnp.float32) ** block_scale(splits[2], (NORB,), ((0, 32),), -0.2, 0.2)), 0.3, 3.0)
    precond = centred(splits[3], (3, NORB, TILE_ORDER), TILE_ORDER ** -0.5, 0.25, ((1, 32),))
    return {"g_less": g_less, "g_great": g_great, "coulomb": coulomb, "precond": precond}


def reference(g_less, g_great, coulomb, precond):
    lesser = g_less.astype(jnp.float32)
    greater = g_great.astype(jnp.float32)
    less_c = lesser[0] + 1j * lesser[1]
    great_c = greater[0] + 1j * greater[1]
    length = 2 * NE
    spec_less = jnp.fft.fft(less_c, length, axis=0)
    spec_great = jnp.fft.fft(jnp.conj(great_c), length, axis=0)
    correl = jnp.fft.ifft(spec_less * jnp.conj(spec_great), axis=0)[:NE]
    polar = (jnp.real(correl) * (0.25 / math.sqrt(NE))).astype(jnp.float32)
    tiles = precond.astype(jnp.float32).reshape(3, N_TILE, TILE_ORDER, TILE_ORDER)
    bare = coulomb[None, :]
    screened = jnp.broadcast_to(bare, (NE, NORB)).astype(jnp.float32)
    for step in range(ITERS):
        resid = bare - screened + bare * polar * screened
        blocks = resid.astype(jnp.bfloat16).astype(jnp.float32).reshape(NE, N_TILE, TILE_ORDER)
        zero_block = jnp.zeros((NE, 1, TILE_ORDER), jnp.float32)
        before = jnp.concatenate([zero_block, blocks[:, :-1]], axis=1)
        after = jnp.concatenate([blocks[:, 1:], zero_block], axis=1)
        corr = jnp.einsum('ebi,bij->ebj', blocks, tiles[0])
        corr = corr + jnp.einsum('ebi,bij->ebj', before, tiles[1])
        corr = corr + jnp.einsum('ebi,bij->ebj', after, tiles[2])
        corr = corr.astype(jnp.bfloat16).reshape(NE, NORB)
        screened = screened + 0.5 * resid + corr.astype(jnp.float32)
    return (polar, screened)
```

```python
import math

import jax
import jax.numpy as jnp
import ml_dtypes
import numpy as np
from jax import lax
from jax.experimental import pallas as pl
from jax.experimental.pallas import tpu as pltpu
from jax.sharding import PartitionSpec as P

ITERS = 2
LANES = 128
VMEM_BYTES = 16 * 1024 * 1024
SLOT = 32


def dft_matrices(total):
    half = total // 2
    angle = 2.0 * np.pi / (2 * total)
    freq = np.arange(half)[:, None]
    rows = []
    for parity in (0, 1):
        at = 2 * np.arange(half)[None, :] + parity
        cos = np.cos(angle * ((freq * at) % (2 * total)))
        sin = np.sin(angle * ((freq * at) % (2 * total)))
        edge = (half * at[0]) % (2 * total)
        sin[0] = np.sin(angle * edge) if parity else np.cos(angle * edge)
        rows.append(np.concatenate([cos, sin], axis=0))
    return rows


def high_low(matrix):
    exact = matrix.astype(np.float32)
    high = exact.astype(ml_dtypes.bfloat16)
    low = (exact - high.astype(np.float32)).astype(ml_dtypes.bfloat16)
    return high, low


def pack_kernel(chunk, less_ref, great_ref, out_ref):
    e_dev, order = less_ref.shape[1], less_ref.shape[2]
    half = e_dev // 2
    row = lax.broadcasted_iota(jnp.int32, (4 * e_dev, 4 * e_dev), 0)
    col = lax.broadcasted_iota(jnp.int32, (4 * e_dev, 4 * e_dev), 1)
    inner = row % e_dev
    source = row - inner + jnp.where(inner < half, 2 * inner, 2 * (inner - half) + 1)
    select = jnp.where(col == source, 1.0, 0.0).astype(jnp.bfloat16)
    rows = jnp.concatenate([less_ref[0], less_ref[1], great_ref[0], great_ref[1]], axis=0)
    sorted_rows = jnp.dot(select, rows, preferred_element_type=jnp.float32)
    lane = lax.broadcasted_iota(jnp.int32, (e_dev, LANES), 1)
    for p in range(out_ref.shape[0]):
        low = chunk * p
        high = min(low + chunk, order) - 1
        first, last = low // LANES, high // LANES
        piece = None
        for q in range(4):
            shift = (SLOT * q - low) % LANES
            part = sorted_rows[e_dev * q : e_dev * (q + 1)]
            moved = pltpu.roll(part[:, LANES * first : LANES * (first + 1)], shift, 1)
            if last > first:
                after = pltpu.roll(part[:, LANES * last : LANES * (last + 1)], shift, 1)
                moved = jnp.where(lane >= SLOT * q + LANES * last - low, after, moved)
            piece = moved if q == 0 else jnp.where(lane >= SLOT * q, moved, piece)
        out_ref[p] = piece.astype(jnp.bfloat16)


def correlate_kernel(scale, data_ref, fwd_ref, back_ref, out_ref):
    blocks, e_dev, _ = data_ref.shape
    half = blocks * e_dev // 2
    spec = []
    for parity in (0, 1):
        rows = data_ref[:, parity * e_dev // 2 : (parity + 1) * e_dev // 2, :].reshape(half, LANES)
        full = jnp.dot(fwd_ref[2 * parity], rows, preferred_element_type=jnp.float32)
        full = full + jnp.dot(fwd_ref[2 * parity + 1], rows, preferred_element_type=jnp.float32)
        spec.append((full[:half], full[half:]))
    (ac_e, as_e), (ac_o, as_o) = spec
    bc_e, bs_e, bc_o, bs_o = (pltpu.roll(x, LANES // 2, 1) for x in (ac_e, as_e, ac_o, as_o))
    edge = lax.broadcasted_iota(jnp.int32, (half, LANES), 0) == 0
    cc = ac_e * bc_e + ac_o * bc_o
    ss = as_e * bs_e + as_o * bs_o
    even_c = jnp.where(edge, 0.5 * cc, cc + ss)
    even_s = jnp.where(edge, 0.5 * ss, as_e * bc_e + as_o * bc_o - ac_e * bs_e - ac_o * bs_o)
    cc = ac_e * bc_o + ac_o * bc_e
    odd_c = jnp.where(edge, 0.5 * cc, cc + as_e * bs_o + as_o * bs_e)
    odd_s = jnp.where(
        edge,
        0.5 * (as_o * bs_e - as_e * bs_o),
        as_e * bc_o + as_o * bc_e - ac_e * bs_o - ac_o * bs_e,
    )
    lane = lax.broadcasted_iota(jnp.int32, (blocks, 8, LANES), 2)
    result = None
    for parity, (c, s) in enumerate(((even_c, even_s), (odd_c, odd_s))):
        c = c - pltpu.roll(c, LANES - SLOT, 1)
        s = s - pltpu.roll(s, LANES - SLOT, 1)
        both = jnp.concatenate([c, s], axis=0).astype(jnp.bfloat16)
        lags = jnp.dot(back_ref[parity], both, preferred_element_type=jnp.float32) * scale
        lags = lags.reshape(blocks, 2, 8, LANES)
        for g in (0, 1):
            slot = 2 * parity + g
            part = lags[:, g]
            if slot == 0:
                result = part
            else:
                result = jnp.where(lane >= SLOT * slot, pltpu.roll(part, SLOT * slot, 2), result)
    out_ref[...] = result.astype(out_ref.dtype)


def store_in_order(sorted_rows, order_ref, out_ref):
    half = sorted_rows.shape[0] // 2
    for tile in range(order_ref.shape[0]):
        lanes = slice(LANES * tile, LANES * (tile + 1))
        order_ref[tile, pl.ds(0, half, stride=2), :] = sorted_rows[:half, lanes]
        order_ref[tile, pl.ds(1, half, stride=2), :] = sorted_rows[half:, lanes]
        out_ref[:, lanes] = order_ref[tile]


def unpack_kernel(chunk, data_ref, bare_ref, polar_ref, sorted_ref, resid_ref, order_ref):
    order = sorted_ref.shape[1]
    lane = lax.broadcasted_iota(jnp.int32, (8, LANES), 1)
    bare = bare_ref[...]
    for g in range(4):
        for tile in range(order // LANES):
            value = None
            p = (LANES * tile) // chunk
            while p < data_ref.shape[0] and chunk * p < LANES * (tile + 1):
                begin = chunk * p - LANES * tile
                moved = pltpu.roll(data_ref[p].astype(jnp.float32), (begin - SLOT * g) % LANES, 1)
                value = moved if value is None else jnp.where(lane >= begin, moved, value)
                p += 1
            lanes = slice(LANES * tile, LANES * (tile + 1))
            sorted_ref[8 * g : 8 * (g + 1), lanes] = value
    polar = sorted_ref[...]
    store_in_order(polar, order_ref, polar_ref)
    resid_ref[...] = (bare * polar * bare).astype(jnp.bfloat16)


def step_kernel(last, parity_ref, own_ref, chip_ref, far_ref, polar_ref, screened_ref, bare_ref, precond_ref, *out_refs):
    bare = bare_ref[...]
    polar = polar_ref[...]
    screened = screened_ref[...] if last else jnp.broadcast_to(bare, polar.shape)
    resid = bare - screened + bare * polar * screened
    even = parity_ref[0] == 0
    chip, far = chip_ref[...], far_ref[...]
    before = jnp.where(even, far, chip)
    after = jnp.where(even, chip, far)
    product = jnp.dot(own_ref[...], precond_ref[0], preferred_element_type=jnp.float32)
    product = product + jnp.dot(before, precond_ref[1], preferred_element_type=jnp.float32)
    product = product + jnp.dot(after, precond_ref[2], preferred_element_type=jnp.float32)
    corr = product.astype(jnp.bfloat16).astype(jnp.float32)
    screened = screened + 0.5 * resid + corr
    if last:
        store_in_order(screened, out_refs[1], out_refs[0])
    else:
        out_refs[0][...] = screened
        out_refs[1][...] = (bare - screened + bare * polar * screened).astype(jnp.bfloat16)


def per_device(g_less, g_great, coulomb, precond):
    e_dev, order = g_less.shape[1:]
    n_energy = lax.axis_size("energy")
    n_tile = lax.axis_size("tile")
    total = e_dev * n_energy
    chunk = -(-order // n_energy)
    vmem = pl.BlockSpec(memory_space=pltpu.VMEM)
    smem = pl.BlockSpec(memory_space=pltpu.SMEM)

    limit = pltpu.CompilerParams(vmem_limit_bytes=VMEM_BYTES)
    matrices = [high_low(m) for m in dft_matrices(total)]
    forward = jnp.asarray(np.stack([part for pair in matrices for part in pair]))
    backward = jnp.asarray(np.stack([np.ascontiguousarray(high.T) for high, _ in matrices]))

    pieces = pl.pallas_call(
        lambda *refs: pack_kernel(chunk, *refs),
        out_shape=jax.ShapeDtypeStruct((n_energy, e_dev, LANES), jnp.bfloat16),
        in_specs=[vmem, vmem],
        out_specs=vmem,
        compiler_params=limit,
    )(g_less, g_great)
    pieces = lax.all_to_all(pieces, "energy", 0, 0, tiled=True)
    scale = 0.25 / math.sqrt(total) * 4.0 / (2 * total)
    lags = pl.pallas_call(
        lambda *refs: correlate_kernel(scale, *refs),
        out_shape=jax.ShapeDtypeStruct((n_energy, 8, LANES), jnp.bfloat16),
        in_specs=[vmem] * 3,
        out_specs=vmem,
        compiler_params=limit,
    )(pieces, forward, backward)
    lags = lax.all_to_all(lags, "energy", 0, 0, tiled=True)
    bare = coulomb[None, :]
    plane = jax.ShapeDtypeStruct((e_dev, order), jnp.float32)
    plane_b = jax.ShapeDtypeStruct((e_dev, order), jnp.bfloat16)
    in_order = pltpu.VMEM((order // LANES, e_dev, LANES), jnp.float32)
    polar, polar_sorted, resid_b = pl.pallas_call(
        lambda *refs: unpack_kernel(chunk, *refs),
        out_shape=(plane, plane, plane_b),
        in_specs=[vmem] * 2,
        out_specs=(vmem,) * 3,
        scratch_shapes=[in_order],
        compiler_params=limit,
    )(lags, bare)
    parity = (lax.axis_index("tile") % 2).astype(jnp.int32).reshape(1)
    screened = polar_sorted
    chip_pairs = [(i, i ^ 1) for i in range(n_tile)]
    far_pairs = [(i, i + 1 if i % 2 else i - 1) for i in range(1, n_tile - 1)]
    for step in range(ITERS):
        last = step == ITERS - 1
        far = lax.ppermute(resid_b, "tile", far_pairs)
        chip = lax.ppermute(resid_b, "tile", chip_pairs)
        out = pl.pallas_call(
            lambda *refs, last=last: step_kernel(last, *refs),
            out_shape=(plane,) if last else (plane, plane_b),
            in_specs=[smem] + [vmem] * 7,
            out_specs=(vmem,) if last else (vmem, vmem),
            scratch_shapes=[in_order] if last else [],
            compiler_params=limit,
        )(parity, resid_b, chip, far, polar_sorted, screened, bare, precond)
        screened = out[0]
        resid_b = out[-1]
    return (polar, screened)


def solution(mesh):
    placed = (
        P(None, "energy", "tile"),
        P(None, "energy", "tile"),
        P("tile"),
        P(None, "tile", None),
    )
    return jax.shard_map(
        per_device,
        mesh=mesh,
        in_specs=placed,
        out_specs=(P("energy", "tile"), P("energy", "tile")),
        check_vma=False,
    )
```

```python
import math

import jax
import jax.numpy as jnp
import ml_dtypes
import numpy as np
from jax import lax
from jax.experimental import pallas as pl
from jax.experimental.pallas import tpu as pltpu
from jax.sharding import PartitionSpec as P

ITERS = 2
LANES = 128
VMEM_BYTES = 16 * 1024 * 1024
SLOT = 32


def dft_matrices(total):
    half = total // 2
    angle = 2.0 * np.pi / (2 * total)
    freq = np.arange(half)[:, None]
    rows = []
    for parity in (0, 1):
        at = 2 * np.arange(half)[None, :] + parity
        cos = np.cos(angle * ((freq * at) % (2 * total)))
        sin = np.sin(angle * ((freq * at) % (2 * total)))
        edge = (half * at[0]) % (2 * total)
        sin[0] = np.sin(angle * edge) if parity else np.cos(angle * edge)
        rows.append(np.concatenate([cos, sin], axis=0))
    return rows


def high_low(matrix):
    exact = matrix.astype(np.float32)
    high = exact.astype(ml_dtypes.bfloat16)
    low = (exact - high.astype(np.float32)).astype(ml_dtypes.bfloat16)
    return high, low


def pack_kernel(chunk, less_hbm, great_hbm, fwd_hbm, back_hbm, out_ref, fwd_ref, back_ref, less_ref, great_ref, sems):
    copies = [
        pltpu.make_async_copy(src, dst, sems.at[n])
        for n, (src, dst) in enumerate(
            ((less_hbm, less_ref), (great_hbm, great_ref), (fwd_hbm, fwd_ref), (back_hbm, back_ref))
        )
    ]
    for copy in copies:
        copy.start()
    e_dev, order = less_ref.shape[1], less_ref.shape[2]
    half = e_dev // 2
    row = lax.broadcasted_iota(jnp.int32, (4 * e_dev, 4 * e_dev), 0)
    col = lax.broadcasted_iota(jnp.int32, (4 * e_dev, 4 * e_dev), 1)
    inner = row % e_dev
    source = row - inner + jnp.where(inner < half, 2 * inner, 2 * (inner - half) + 1)
    select = jnp.where(col == source, 1.0, 0.0).astype(jnp.bfloat16)
    lane = lax.broadcasted_iota(jnp.int32, (e_dev, LANES), 1)
    in_slot = lax.broadcasted_iota(jnp.int32, (8, LANES), 1) % SLOT
    spare = SLOT - chunk
    copies[0].wait()
    copies[1].wait()
    rows = jnp.concatenate([less_ref[0], less_ref[1], great_ref[0], great_ref[1]], axis=0)
    sorted_rows = jnp.dot(select, rows, preferred_element_type=jnp.float32)
    for p in range(out_ref.shape[0]):
        low = chunk * p
        high = min(low + chunk, order) - 1
        first, last = low // LANES, high // LANES
        piece = None
        for q in range(4):
            shift = (SLOT * q - low) % LANES
            part = sorted_rows[e_dev * q : e_dev * (q + 1)]
            moved = pltpu.roll(part[:, LANES * first : LANES * (first + 1)], shift, 1)
            if last > first:
                after = pltpu.roll(part[:, LANES * last : LANES * (last + 1)], shift, 1)
                moved = jnp.where(lane >= SLOT * q + LANES * last - low, after, moved)
            piece = moved if q == 0 else jnp.where(lane >= SLOT * q, moved, piece)
        rest = piece[24:]
        full = [
            jnp.where(in_slot < chunk, piece[8 * g : 8 * (g + 1)], pltpu.roll(rest, chunk - spare * g, 1))
            for g in range(3)
        ]
        out_ref[p] = jnp.concatenate(full, axis=0).astype(jnp.bfloat16)
    copies[2].wait()
    copies[3].wait()


def correlate_kernel(chunk, scale, data_ref, fwd_ref, back_ref, out_ref):
    blocks = data_ref.shape[0]
    half = fwd_ref.shape[2]
    in_slot = lax.broadcasted_iota(jnp.int32, (blocks, 8, LANES), 2) % SLOT
    spare = SLOT - chunk
    packed = [data_ref[:, 8 * g : 8 * (g + 1), :].astype(jnp.float32) for g in range(3)]
    rest = None
    for g in range(3):
        moved = pltpu.roll(packed[g], LANES - chunk + spare * g, 2)
        rest = moved if g == 0 else jnp.where(in_slot >= spare * g, moved, rest)
    spec = []
    for parity in (0, 1):
        rows = packed[:2] if parity == 0 else [packed[2], rest]
        rows = jnp.concatenate(rows, axis=1).reshape(half, LANES).astype(jnp.bfloat16)
        full = jnp.dot(fwd_ref[2 * parity], rows, preferred_element_type=jnp.float32)
        full = full + jnp.dot(fwd_ref[2 * parity + 1], rows, preferred_element_type=jnp.float32)
        spec.append((full[:half], full[half:]))
    (ac_e, as_e), (ac_o, as_o) = spec
    bc_e, bs_e, bc_o, bs_o = (pltpu.roll(x, LANES // 2, 1) for x in (ac_e, as_e, ac_o, as_o))
    edge = lax.broadcasted_iota(jnp.int32, (half, LANES), 0) == 0
    cc = ac_e * bc_e + ac_o * bc_o
    ss = as_e * bs_e + as_o * bs_o
    even_c = jnp.where(edge, 0.5 * cc, cc + ss)
    even_s = jnp.where(edge, 0.5 * ss, as_e * bc_e + as_o * bc_o - ac_e * bs_e - ac_o * bs_o)
    cc = ac_e * bc_o + ac_o * bc_e
    odd_c = jnp.where(edge, 0.5 * cc, cc + as_e * bs_o + as_o * bs_e)
    odd_s = jnp.where(
        edge,
        0.5 * (as_o * bs_e - as_e * bs_o),
        as_e * bc_o + as_o * bc_e - ac_e * bs_o - ac_o * bs_e,
    )
    lane = lax.broadcasted_iota(jnp.int32, (blocks, 8, LANES), 2)
    result = None
    for parity, (c, s) in enumerate(((even_c, even_s), (odd_c, odd_s))):
        c = c - pltpu.roll(c, LANES - SLOT, 1)
        s = s - pltpu.roll(s, LANES - SLOT, 1)
        both = jnp.concatenate([c, s], axis=0).astype(jnp.bfloat16)
        lags = jnp.dot(back_ref[parity], both, preferred_element_type=jnp.float32) * scale
        lags = lags.reshape(blocks, 2, 8, LANES)
        for g in (0, 1):
            slot = 2 * parity + g
            part = lags[:, g]
            if slot == 0:
                result = part
            else:
                result = jnp.where(lane >= SLOT * slot, pltpu.roll(part, SLOT * slot, 2), result)
    out_ref[...] = result.astype(out_ref.dtype)


def store_in_order(sorted_rows, order_ref, out_ref):
    half = sorted_rows.shape[0] // 2
    for tile in range(order_ref.shape[0]):
        lanes = slice(LANES * tile, LANES * (tile + 1))
        order_ref[tile, pl.ds(0, half, stride=2), :] = sorted_rows[:half, lanes]
        order_ref[tile, pl.ds(1, half, stride=2), :] = sorted_rows[half:, lanes]
        out_ref[:, lanes] = order_ref[tile]


def unpack_kernel(chunk, data_ref, bare_ref, sorted_ref, resid_ref):
    order = sorted_ref.shape[1]
    lane = lax.broadcasted_iota(jnp.int32, (8, LANES), 1)
    for g in range(4):
        for tile in range(order // LANES):
            value = None
            p = (LANES * tile) // chunk
            while p < data_ref.shape[0] and chunk * p < LANES * (tile + 1):
                begin = chunk * p - LANES * tile
                moved = pltpu.roll(data_ref[p].astype(jnp.float32), (begin - SLOT * g) % LANES, 1)
                value = moved if value is None else jnp.where(lane >= begin, moved, value)
                p += 1
            sorted_ref[8 * g : 8 * (g + 1), LANES * tile : LANES * (tile + 1)] = value
    bare = bare_ref[...]
    resid_ref[...] = (bare * sorted_ref[...] * bare).astype(jnp.bfloat16)


def order_kernel(sorted_ref, out_ref, order_ref):
    store_in_order(sorted_ref[...], order_ref, out_ref)


def step_kernel(last, parity_ref, own_ref, chip_ref, far_ref, polar_ref, screened_ref, bare_ref, precond_ref, *out_refs):
    bare = bare_ref[...]
    polar = polar_ref[...]
    screened = screened_ref[...] if last else jnp.broadcast_to(bare, polar.shape)
    resid = bare - screened + bare * polar * screened
    even = parity_ref[0] == 0
    chip, far = chip_ref[...], far_ref[...]
    before = jnp.where(even, far, chip)
    after = jnp.where(even, chip, far)
    product = jnp.dot(own_ref[...], precond_ref[0], preferred_element_type=jnp.float32)
    product = product + jnp.dot(before, precond_ref[1], preferred_element_type=jnp.float32)
    product = product + jnp.dot(after, precond_ref[2], preferred_element_type=jnp.float32)
    corr = product.astype(jnp.bfloat16).astype(jnp.float32)
    screened = screened + 0.5 * resid + corr
    if last:
        store_in_order(screened, out_refs[1], out_refs[0])
    else:
        out_refs[0][...] = screened
        out_refs[1][...] = (bare - screened + bare * polar * screened).astype(jnp.bfloat16)


def per_device(g_less, g_great, coulomb, precond):
    e_dev, order = g_less.shape[1:]
    n_energy = lax.axis_size("energy")
    n_tile = lax.axis_size("tile")
    total = e_dev * n_energy
    chunk = -(-order // n_energy)
    vmem = pl.BlockSpec(memory_space=pltpu.VMEM)
    smem = pl.BlockSpec(memory_space=pltpu.SMEM)

    limit = pltpu.CompilerParams(vmem_limit_bytes=VMEM_BYTES)
    matrices = [high_low(m) for m in dft_matrices(total)]
    forward = jnp.asarray(np.stack([part for pair in matrices for part in pair]))
    backward = jnp.asarray(np.stack([np.ascontiguousarray(high.T) for high, _ in matrices]))

    hbm = pl.BlockSpec(memory_space=pltpu.HBM)
    pieces, forward, backward = pl.pallas_call(
        lambda *refs: pack_kernel(chunk, *refs),
        out_shape=(
            jax.ShapeDtypeStruct((n_energy, 24, LANES), jnp.bfloat16),
            jax.ShapeDtypeStruct(forward.shape, jnp.bfloat16),
            jax.ShapeDtypeStruct(backward.shape, jnp.bfloat16),
        ),
        in_specs=[hbm] * 4,
        out_specs=(vmem,) * 3,
        scratch_shapes=[pltpu.VMEM(g_less.shape, jnp.bfloat16)] * 2 + [pltpu.SemaphoreType.DMA((4,))],
        compiler_params=limit,
    )(*(pltpu.with_memory_space_constraint(x, pltpu.HBM) for x in (g_less, g_great, forward, backward)))
    pieces = lax.all_to_all(pieces, "energy", 0, 0, tiled=True)
    scale = 0.25 / math.sqrt(total) * 4.0 / (2 * total)
    lags = pl.pallas_call(
        lambda *refs: correlate_kernel(chunk, scale, *refs),
        out_shape=jax.ShapeDtypeStruct((n_energy, 8, LANES), jnp.bfloat16),
        in_specs=[vmem] * 3,
        out_specs=vmem,
        compiler_params=limit,
    )(pieces, forward, backward)
    lags = lax.all_to_all(lags, "energy", 0, 0, tiled=True)
    bare = coulomb[None, :]
    plane = jax.ShapeDtypeStruct((e_dev, order), jnp.float32)
    plane_b = jax.ShapeDtypeStruct((e_dev, order), jnp.bfloat16)
    in_order = pltpu.VMEM((order // LANES, e_dev, LANES), jnp.float32)
    polar_sorted, resid_b = pl.pallas_call(
        lambda *refs: unpack_kernel(chunk, *refs),
        out_shape=(plane, plane_b),
        in_specs=[vmem] * 2,
        out_specs=(vmem,) * 2,
        compiler_params=limit,
    )(lags, bare)
    polar = pl.pallas_call(
        order_kernel,
        out_shape=plane,
        in_specs=[vmem],
        out_specs=vmem,
        scratch_shapes=[in_order],
        compiler_params=limit,
        cost_estimate=pl.CostEstimate(flops=1000, bytes_accessed=1000, transcendentals=0),
    )(polar_sorted)
    parity = (lax.axis_index("tile") % 2).astype(jnp.int32).reshape(1)
    screened = polar_sorted
    chip_pairs = [(i, i ^ 1) for i in range(n_tile)]
    far_pairs = [(i, i + 1 if i % 2 else i - 1) for i in range(1, n_tile - 1)]
    for step in range(ITERS):
        last = step == ITERS - 1
        far = lax.ppermute(resid_b, "tile", far_pairs)
        chip = lax.ppermute(resid_b, "tile", chip_pairs)
        out = pl.pallas_call(
            lambda *refs, last=last: step_kernel(last, *refs),
            out_shape=(plane,) if last else (plane, plane_b),
            in_specs=[smem] + [vmem] * 7,
            out_specs=(vmem,) if last else (vmem, vmem),
            scratch_shapes=[in_order] if last else [],
            compiler_params=limit,
        )(parity, resid_b, chip, far, polar_sorted, screened, bare, precond)
        screened = out[0]
        resid_b = out[-1]
    return (polar, screened)


def solution(mesh):
    placed = (
        P(None, "energy", "tile"),
        P(None, "energy", "tile"),
        P("tile"),
        P(None, "tile", None),
    )
    return jax.shard_map(
        per_device,
        mesh=mesh,
        in_specs=placed,
        out_specs=(P("energy", "tile"), P("energy", "tile")),
        check_vma=False,
    )
```

```python
import math

import jax
import jax.numpy as jnp
import ml_dtypes
import numpy as np
from jax import lax
from jax.experimental import pallas as pl
from jax.experimental.pallas import tpu as pltpu
from jax.sharding import PartitionSpec as P

ITERS = 2
LANES = 128
VMEM_BYTES = 16 * 1024 * 1024
SLOT = 32


def dft_matrices(total):
    half = total // 2
    angle = 2.0 * np.pi / (2 * total)
    freq = np.arange(half)[:, None]
    rows = []
    for parity in (0, 1):
        at = 2 * np.arange(half)[None, :] + parity
        cos = np.cos(angle * ((freq * at) % (2 * total)))
        sin = np.sin(angle * ((freq * at) % (2 * total)))
        edge = (half * at[0]) % (2 * total)
        sin[0] = np.sin(angle * edge) if parity else np.cos(angle * edge)
        rows.append(np.concatenate([cos, sin], axis=0))
    return rows


def high_low(matrix):
    exact = matrix.astype(np.float32)
    high = exact.astype(ml_dtypes.bfloat16)
    low = (exact - high.astype(np.float32)).astype(ml_dtypes.bfloat16)
    return high, low


def pack_kernel(chunk, less_hbm, great_hbm, fwd_hbm, out_ref, fwd_ref, less_ref, great_ref, sems):
    copies = [
        pltpu.make_async_copy(src, dst, sems.at[n])
        for n, (src, dst) in enumerate(
            ((less_hbm, less_ref), (great_hbm, great_ref), (fwd_hbm, fwd_ref))
        )
    ]
    for copy in copies:
        copy.start()
    e_dev, order = less_ref.shape[1], less_ref.shape[2]
    half = e_dev // 2
    row = lax.broadcasted_iota(jnp.int32, (4 * e_dev, 4 * e_dev), 0)
    col = lax.broadcasted_iota(jnp.int32, (4 * e_dev, 4 * e_dev), 1)
    inner = row % e_dev
    source = row - inner + jnp.where(inner < half, 2 * inner, 2 * (inner - half) + 1)
    select = jnp.where(col == source, 1.0, 0.0).astype(jnp.bfloat16)
    lane = lax.broadcasted_iota(jnp.int32, (e_dev, LANES), 1)
    in_slot = lax.broadcasted_iota(jnp.int32, (8, LANES), 1) % SLOT
    spare = SLOT - chunk
    copies[0].wait()
    copies[1].wait()
    rows = jnp.concatenate([less_ref[0], less_ref[1], great_ref[0], great_ref[1]], axis=0)
    sorted_rows = jnp.dot(select, rows, preferred_element_type=jnp.float32)
    for p in range(out_ref.shape[0]):
        low = chunk * p
        high = min(low + chunk, order) - 1
        first, last = low // LANES, high // LANES
        piece = None
        for q in range(4):
            shift = (SLOT * q - low) % LANES
            part = sorted_rows[e_dev * q : e_dev * (q + 1)]
            moved = pltpu.roll(part[:, LANES * first : LANES * (first + 1)], shift, 1)
            if last > first:
                after = pltpu.roll(part[:, LANES * last : LANES * (last + 1)], shift, 1)
                moved = jnp.where(lane >= SLOT * q + LANES * last - low, after, moved)
            piece = moved if q == 0 else jnp.where(lane >= SLOT * q, moved, piece)
        rest = piece[24:]
        full = [
            jnp.where(in_slot < chunk, piece[8 * g : 8 * (g + 1)], pltpu.roll(rest, chunk - spare * g, 1))
            for g in range(3)
        ]
        out_ref[p] = jnp.concatenate(full, axis=0).astype(jnp.bfloat16)
    copies[2].wait()


def correlate_kernel(chunk, scale, data_ref, fwd_ref, back_hbm, out_ref, back_ref, sem):
    copy = pltpu.make_async_copy(back_hbm, back_ref, sem)
    copy.start()
    blocks = data_ref.shape[0]
    half = fwd_ref.shape[2] // 2
    in_slot = lax.broadcasted_iota(jnp.int32, (blocks, 8, LANES), 2) % SLOT
    spare = SLOT - chunk
    packed = [data_ref[:, 8 * g : 8 * (g + 1), :].astype(jnp.float32) for g in range(3)]
    rest = None
    for g in range(3):
        moved = pltpu.roll(packed[g], LANES - chunk + spare * g, 2)
        rest = moved if g == 0 else jnp.where(in_slot >= spare * g, moved, rest)
    spec = []
    for parity in (0, 1):
        rows = packed[:2] if parity == 0 else [packed[2], rest]
        rows = jnp.concatenate(rows, axis=1).reshape(half, LANES).astype(jnp.bfloat16)
        rows = jnp.concatenate([rows, rows], axis=0)
        full = jnp.dot(fwd_ref[parity], rows, preferred_element_type=jnp.float32)
        spec.append((full[:half], full[half:]))
    (ac_e, as_e), (ac_o, as_o) = spec
    bc_e, bs_e, bc_o, bs_o = (pltpu.roll(x, LANES // 2, 1) for x in (ac_e, as_e, ac_o, as_o))
    edge = lax.broadcasted_iota(jnp.int32, (half, LANES), 0) == 0
    cc = ac_e * bc_e + ac_o * bc_o
    ss = as_e * bs_e + as_o * bs_o
    even_c = jnp.where(edge, 0.5 * cc, cc + ss)
    even_s = jnp.where(edge, 0.5 * ss, as_e * bc_e + as_o * bc_o - ac_e * bs_e - ac_o * bs_o)
    cc = ac_e * bc_o + ac_o * bc_e
    odd_c = jnp.where(edge, 0.5 * cc, cc + as_e * bs_o + as_o * bs_e)
    odd_s = jnp.where(
        edge,
        0.5 * (as_o * bs_e - as_e * bs_o),
        as_e * bc_o + as_o * bc_e - ac_e * bs_o - ac_o * bs_e,
    )
    lane = lax.broadcasted_iota(jnp.int32, (blocks, 8, LANES), 2)
    result = None
    copy.wait()
    for parity, (c, s) in enumerate(((even_c, even_s), (odd_c, odd_s))):
        c = c - pltpu.roll(c, LANES - SLOT, 1)
        s = s - pltpu.roll(s, LANES - SLOT, 1)
        both = jnp.concatenate([c, s], axis=0).astype(jnp.bfloat16)
        lags = jnp.dot(back_ref[parity], both, preferred_element_type=jnp.float32) * scale
        lags = lags.reshape(blocks, 2, 8, LANES)
        for g in (0, 1):
            slot = 2 * parity + g
            part = lags[:, g]
            if slot == 0:
                result = part
            else:
                result = jnp.where(lane >= SLOT * slot, pltpu.roll(part, SLOT * slot, 2), result)
    out_ref[...] = result.astype(out_ref.dtype)


def tile_copy(refs, tile):
    out_hbm, order_ref, sems = refs
    return pltpu.make_async_copy(
        order_ref.at[tile], out_hbm.at[:, LANES * tile : LANES * (tile + 1)], sems.at[tile]
    )


def store_in_order(sorted_rows, refs, at):
    half = sorted_rows.shape[0] // 2
    for n in range(sorted_rows.shape[1] // LANES):
        lanes = slice(LANES * n, LANES * (n + 1))
        tile = at // LANES + n
        refs[1][tile, pl.ds(0, half, stride=2), :] = sorted_rows[:half, lanes]
        refs[1][tile, pl.ds(1, half, stride=2), :] = sorted_rows[half:, lanes]
        tile_copy(refs, tile).start()


def wait_in_order(refs):
    for tile in range(refs[1].shape[0]):
        tile_copy(refs, tile).wait()


def unpack_kernel(chunk, data_ref, bare_ref, sorted_ref, resid_ref):
    order = sorted_ref.shape[1]
    lane = lax.broadcasted_iota(jnp.int32, (8, LANES), 1)
    for g in range(4):
        for tile in range(order // LANES):
            value = None
            p = (LANES * tile) // chunk
            while p < data_ref.shape[0] and chunk * p < LANES * (tile + 1):
                begin = chunk * p - LANES * tile
                moved = pltpu.roll(data_ref[p].astype(jnp.float32), (begin - SLOT * g) % LANES, 1)
                value = moved if value is None else jnp.where(lane >= begin, moved, value)
                p += 1
            sorted_ref[8 * g : 8 * (g + 1), LANES * tile : LANES * (tile + 1)] = value
    bare = bare_ref[...]
    resid_ref[...] = (bare * sorted_ref[...] * bare).astype(jnp.bfloat16)


def order_kernel(sorted_ref, *refs):
    store_in_order(sorted_ref[...], refs, 0)
    wait_in_order(refs)


def near_kernel(parity_ref, own_ref, chip_ref, precond_ref, out_ref):
    which = 2 - parity_ref[0]
    out_ref[...] = jnp.dot(own_ref[...], precond_ref[0], preferred_element_type=jnp.float32) + jnp.dot(
        chip_ref[...], precond_ref[which], preferred_element_type=jnp.float32
    )


def step_kernel(last, parity_ref, near_ref, far_ref, polar_ref, screened_ref, bare_ref, precond_ref, *refs):
    which = 1 + parity_ref[0]
    far = far_ref[...]
    width = 256 if last else far.shape[1]
    for at in range(0, far.shape[1], width):
        lanes = slice(at, at + width)
        bare, polar = bare_ref[:, lanes], polar_ref[:, lanes]
        screened = screened_ref[:, lanes] if last else jnp.broadcast_to(bare, polar.shape)
        resid = bare - screened + bare * polar * screened
        product = near_ref[:, lanes] + jnp.dot(far, precond_ref[which, :, lanes], preferred_element_type=jnp.float32)
        corr = product.astype(jnp.bfloat16).astype(jnp.float32)
        screened = screened + 0.5 * resid + corr
        if last:
            store_in_order(screened, refs, at)
        else:
            refs[0][:, lanes] = screened
            refs[1][:, lanes] = (bare - screened + bare * polar * screened).astype(jnp.bfloat16)
    if last:
        wait_in_order(refs)


def per_device(g_less, g_great, coulomb, precond):
    e_dev, order = g_less.shape[1:]
    n_energy = lax.axis_size("energy")
    n_tile = lax.axis_size("tile")
    total = e_dev * n_energy
    chunk = -(-order // n_energy)
    vmem = pl.BlockSpec(memory_space=pltpu.VMEM)
    smem = pl.BlockSpec(memory_space=pltpu.SMEM)

    limit = pltpu.CompilerParams(vmem_limit_bytes=VMEM_BYTES)
    matrices = [high_low(m) for m in dft_matrices(total)]
    forward = jnp.asarray(np.stack([np.concatenate(pair, axis=1) for pair in matrices]))
    backward = jnp.asarray(np.stack([np.ascontiguousarray(high.T) for high, _ in matrices]))

    hbm = pl.BlockSpec(memory_space=pltpu.HBM)
    g_less, g_great, forward, backward = (
        pltpu.with_memory_space_constraint(x, pltpu.HBM) for x in (g_less, g_great, forward, backward)
    )
    pieces, forward = pl.pallas_call(
        lambda *refs: pack_kernel(chunk, *refs),
        out_shape=(
            jax.ShapeDtypeStruct((n_energy, 24, LANES), jnp.bfloat16),
            jax.ShapeDtypeStruct(forward.shape, jnp.bfloat16),
        ),
        in_specs=[hbm] * 3,
        out_specs=(vmem,) * 2,
        scratch_shapes=[pltpu.VMEM(g_less.shape, jnp.bfloat16)] * 2 + [pltpu.SemaphoreType.DMA((3,))],
        compiler_params=limit,
    )(g_less, g_great, forward)
    pieces = lax.all_to_all(pieces, "energy", 0, 0, tiled=True)
    scale = 0.25 / math.sqrt(total) * 4.0 / (2 * total)
    lags = pl.pallas_call(
        lambda *refs: correlate_kernel(chunk, scale, *refs),
        out_shape=jax.ShapeDtypeStruct((n_energy, 8, LANES), jnp.bfloat16),
        in_specs=[vmem, vmem, hbm],
        out_specs=vmem,
        scratch_shapes=[pltpu.VMEM(backward.shape, jnp.bfloat16), pltpu.SemaphoreType.DMA(())],
        compiler_params=limit,
    )(pieces, forward, backward)
    lags = lax.all_to_all(lags, "energy", 0, 0, tiled=True)
    bare = coulomb[None, :]
    plane = jax.ShapeDtypeStruct((e_dev, order), jnp.float32)
    plane_b = jax.ShapeDtypeStruct((e_dev, order), jnp.bfloat16)
    in_order = [
        pltpu.VMEM((order // LANES, e_dev, LANES), jnp.float32),
        pltpu.SemaphoreType.DMA((order // LANES,)),
    ]
    polar_sorted, resid_b = pl.pallas_call(
        lambda *refs: unpack_kernel(chunk, *refs),
        out_shape=(plane, plane_b),
        in_specs=[vmem] * 2,
        out_specs=(vmem,) * 2,
        compiler_params=limit,
    )(lags, bare)
    polar = pl.pallas_call(
        order_kernel,
        out_shape=plane,
        in_specs=[vmem],
        out_specs=hbm,
        scratch_shapes=in_order,
        compiler_params=limit,
        cost_estimate=pl.CostEstimate(flops=1000, bytes_accessed=1000, transcendentals=0),
    )(polar_sorted)
    parity = (lax.axis_index("tile") % 2).astype(jnp.int32).reshape(1)
    screened = polar_sorted
    chip_pairs = [(i, i ^ 1) for i in range(n_tile)]
    far_pairs = [(i, i + 1 if i % 2 else i - 1) for i in range(1, n_tile - 1)]
    for step in range(ITERS):
        last = step == ITERS - 1
        far = lax.ppermute(resid_b, "tile", far_pairs)
        chip = lax.ppermute(resid_b, "tile", chip_pairs)
        near = pl.pallas_call(
            near_kernel,
            out_shape=plane,
            in_specs=[smem] + [vmem] * 3,
            out_specs=vmem,
            compiler_params=limit,
        )(parity, resid_b, chip, precond)
        out = pl.pallas_call(
            lambda *refs, last=last: step_kernel(last, *refs),
            out_shape=(plane,) if last else (plane, plane_b),
            in_specs=[smem] + [vmem] * 6,
            out_specs=(hbm,) if last else (vmem, vmem),
            scratch_shapes=in_order if last else [],
            compiler_params=limit,
        )(parity, near, far, polar_sorted, screened, bare, precond)
        screened = out[0]
        resid_b = out[-1]
    return (polar, screened)


def solution(mesh):
    placed = (
        P(None, "energy", "tile"),
        P(None, "energy", "tile"),
        P("tile"),
        P(None, "tile", None),
    )
    return jax.shard_map(
        per_device,
        mesh=mesh,
        in_specs=placed,
        out_specs=(P("energy", "tile"), P("energy", "tile")),
        check_vma=False,
    )
```

```python
import math

import jax
import jax.numpy as jnp
import ml_dtypes
import numpy as np
from jax import lax
from jax.experimental import pallas as pl
from jax.experimental.pallas import tpu as pltpu
from jax.sharding import PartitionSpec as P

ITERS = 2
LANES = 128
VMEM_BYTES = 16 * 1024 * 1024
SLOT = 32


def dft_matrices(total):
    rows, length = total // 4, 2 * total
    freq = np.arange(rows)[:, None]
    matrices = []
    for r in range(4):
        turn = (freq * (4 * np.arange(rows)[None, :] + r)) % length
        cos, sin = np.cos(2.0 * np.pi * turn / length), np.sin(2.0 * np.pi * turn / length)
        sin[0] = 1.0 - 2.0 * (np.arange(rows) % 2)
        matrices.append(np.concatenate([cos, sin], axis=0))
    return matrices


def high_low(matrix):
    exact = matrix.astype(np.float32)
    high = exact.astype(ml_dtypes.bfloat16)
    low = (exact - high.astype(np.float32)).astype(ml_dtypes.bfloat16)
    return high, low


def pack_kernel(chunk, less_hbm, great_hbm, fwd_hbm, back_hbm, out_ref, fwd_ref, back_ref, less_ref, great_ref, sems):
    copies = [
        pltpu.make_async_copy(src, dst, sems.at[n])
        for n, (src, dst) in enumerate(
            ((less_hbm, less_ref), (great_hbm, great_ref), (fwd_hbm, fwd_ref), (back_hbm, back_ref))
        )
    ]
    for copy in copies:
        copy.start()
    e_dev, order = less_ref.shape[1], less_ref.shape[2]
    row = lax.broadcasted_iota(jnp.int32, (4 * e_dev, 4 * e_dev), 0)
    col = lax.broadcasted_iota(jnp.int32, (4 * e_dev, 4 * e_dev), 1)
    inner = row % e_dev
    source = row - inner + 4 * (inner % 8) + inner // 8
    select = jnp.where(col == source, 1.0, 0.0).astype(jnp.bfloat16)
    lane = lax.broadcasted_iota(jnp.int32, (e_dev, LANES), 1)
    in_slot = lax.broadcasted_iota(jnp.int32, (8, LANES), 1) % SLOT
    spare = SLOT - chunk
    copies[0].wait()
    copies[1].wait()
    rows = jnp.concatenate([less_ref[0], less_ref[1], great_ref[0], great_ref[1]], axis=0)
    sorted_rows = jnp.dot(select, rows, preferred_element_type=jnp.float32)
    for p in range(out_ref.shape[0]):
        low = chunk * p
        high = min(low + chunk, order) - 1
        first, last = low // LANES, high // LANES
        piece = None
        for q in range(4):
            shift = (SLOT * q - low) % LANES
            part = sorted_rows[e_dev * q : e_dev * (q + 1)]
            moved = pltpu.roll(part[:, LANES * first : LANES * (first + 1)], shift, 1)
            if last > first:
                after = pltpu.roll(part[:, LANES * last : LANES * (last + 1)], shift, 1)
                moved = jnp.where(lane >= SLOT * q + LANES * last - low, after, moved)
            piece = moved if q == 0 else jnp.where(lane >= SLOT * q, moved, piece)
        rest = piece[24:]
        full = [
            jnp.where(in_slot < chunk, piece[8 * g : 8 * (g + 1)], pltpu.roll(rest, chunk - spare * g, 1))
            for g in range(3)
        ]
        out_ref[p] = jnp.concatenate(full, axis=0).astype(jnp.bfloat16)
    copies[2].wait()
    copies[3].wait()


def product(a, b):
    return a[0] * b[0] + a[1] * b[1], a[1] * b[0] - a[0] * b[1]


def correlate_kernel(chunk, scale, data_ref, fwd_ref, back_ref, out_ref):
    blocks = data_ref.shape[0]
    rows = back_ref.shape[1]
    in_slot = lax.broadcasted_iota(jnp.int32, (blocks, 8, LANES), 2) % SLOT
    spare = SLOT - chunk
    packed = [data_ref[:, 8 * g : 8 * (g + 1), :].astype(jnp.float32) for g in range(3)]
    rest = None
    for g in range(3):
        moved = pltpu.roll(packed[g], LANES - chunk + spare * g, 2)
        rest = moved if g == 0 else jnp.where(in_slot >= spare * g, moved, rest)
    c, s = [], []
    for r in range(4):
        energies = (packed + [rest])[r].reshape(rows, LANES).astype(jnp.bfloat16)
        full = jnp.dot(fwd_ref[r, :, :rows], energies, preferred_element_type=jnp.float32)
        full = full + jnp.dot(fwd_ref[r, :, rows:], energies, preferred_element_type=jnp.float32)
        c.append(full[:rows])
        s.append(full[rows:])

    def times_other(spectrum):
        return product(spectrum, [pltpu.roll(x, LANES // 2, 1) for x in spectrum])

    c02, c02m, c13, c13m = c[0] + c[2], c[0] - c[2], c[1] + c[3], c[1] - c[3]
    s02, s02m, s13, s13m = s[0] + s[2], s[0] - s[2], s[1] + s[3], s[1] - s[3]
    low, low_i = times_other((c02 + c13, s02 + s13))
    top, top_i = times_other((c02 - c13, s13 - s02))
    under, under_i = times_other((c02m + s13m, c13m - s02m))
    over, over_i = times_other((c02m - s13m, c13m + s02m))
    pairs = (
        (low + top + under + over, low_i - top_i - under_i + over_i),
        (low - top + under_i + over_i, low_i + top_i + under - over),
        (low + top - under - over, low_i - top_i + under_i - over_i),
        (low - top - under_i - over_i, low_i + top_i - under + over),
    )
    root = math.sqrt(0.5)
    c0, z0 = [x[:8] for x in c], [x[:8] for x in s]
    zero = jnp.zeros_like(c0[0])
    first, _ = times_other((c0[0] + c0[1] + c0[2] + c0[3], zero))
    final, _ = times_other((c0[0] - c0[1] + c0[2] - c0[3], zero))
    mid, mid_i = times_other((c0[0] - c0[2], c0[1] - c0[3]))
    turned_sum, turned_dif = root * (z0[1] + z0[3]), root * (z0[1] - z0[3])
    quarter, quarter_i = times_other((z0[0] + turned_dif, turned_sum + z0[2]))
    three, three_i = times_other((z0[0] - turned_dif, turned_sum - z0[2]))
    edges = (
        (0.5 * (first + final) + mid, quarter + three),
        (0.5 * (first - final) + mid_i, root * (quarter - three + quarter_i + three_i)),
        (0.5 * (first + final) - mid, quarter_i - three_i),
        (0.5 * (first - final) - mid_i, root * (three - quarter + quarter_i + three_i)),
    )
    edge = lax.broadcasted_iota(jnp.int32, (8, LANES), 0) == 0
    lane = lax.broadcasted_iota(jnp.int32, (blocks, 8, LANES), 2)
    result = None
    for r in range(4):
        both = []
        for value, at_edge in zip(pairs[r], edges[r]):
            value = jnp.concatenate([jnp.where(edge, at_edge, value[:8]), value[8:]], axis=0)
            both.append(value - pltpu.roll(value, LANES - SLOT, 1))
        both = jnp.concatenate(both, axis=0).astype(jnp.bfloat16)
        lags = jnp.dot(back_ref[r], both, preferred_element_type=jnp.float32) * scale
        lags = lags.reshape(blocks, 8, LANES)
        result = lags if r == 0 else jnp.where(lane >= SLOT * r, pltpu.roll(lags, SLOT * r, 2), result)
    out_ref[...] = result.astype(out_ref.dtype)


def tile_copy(refs, tile):
    out_hbm, order_ref, sems = refs
    return pltpu.make_async_copy(
        order_ref.at[tile], out_hbm.at[:, LANES * tile : LANES * (tile + 1)], sems.at[tile]
    )


def store_in_order(sorted_rows, refs, at):
    for n in range(sorted_rows.shape[1] // LANES):
        lanes = slice(LANES * n, LANES * (n + 1))
        tile = at // LANES + n
        for r in range(4):
            refs[1][tile, pl.ds(r, 8, stride=4), :] = sorted_rows[8 * r : 8 * (r + 1), lanes]
        tile_copy(refs, tile).start()


def wait_in_order(refs):
    for tile in range(refs[1].shape[0]):
        tile_copy(refs, tile).wait()


def unpack_kernel(chunk, data_ref, bare_ref, sorted_ref, resid_ref):
    order = sorted_ref.shape[1]
    lane = lax.broadcasted_iota(jnp.int32, (8, LANES), 1)
    for g in range(4):
        for tile in range(order // LANES):
            value = None
            p = (LANES * tile) // chunk
            while p < data_ref.shape[0] and chunk * p < LANES * (tile + 1):
                begin = chunk * p - LANES * tile
                moved = pltpu.roll(data_ref[p].astype(jnp.float32), (begin - SLOT * g) % LANES, 1)
                value = moved if value is None else jnp.where(lane >= begin, moved, value)
                p += 1
            sorted_ref[8 * g : 8 * (g + 1), LANES * tile : LANES * (tile + 1)] = value
    bare = bare_ref[...]
    resid_ref[...] = (bare * sorted_ref[...] * bare).astype(jnp.bfloat16)


def order_kernel(sorted_ref, *refs):
    store_in_order(sorted_ref[...], refs, 0)
    wait_in_order(refs)


def near_kernel(parity_ref, own_ref, chip_ref, precond_ref, out_ref):
    which = 2 - parity_ref[0]
    out_ref[...] = jnp.dot(own_ref[...], precond_ref[0], preferred_element_type=jnp.float32) + jnp.dot(
        chip_ref[...], precond_ref[which], preferred_element_type=jnp.float32
    )


def step_kernel(last, parity_ref, near_ref, far_ref, polar_ref, screened_ref, bare_ref, precond_ref, *refs):
    which = 1 + parity_ref[0]
    far = far_ref[...]
    width = 256 if last else far.shape[1]
    for at in range(0, far.shape[1], width):
        lanes = slice(at, at + width)
        bare, polar = bare_ref[:, lanes], polar_ref[:, lanes]
        screened = screened_ref[:, lanes] if last else jnp.broadcast_to(bare, polar.shape)
        resid = bare - screened + bare * polar * screened
        product = near_ref[:, lanes] + jnp.dot(far, precond_ref[which, :, lanes], preferred_element_type=jnp.float32)
        corr = product.astype(jnp.bfloat16).astype(jnp.float32)
        screened = screened + 0.5 * resid + corr
        if last:
            store_in_order(screened, refs, at)
        else:
            refs[0][:, lanes] = screened
            refs[1][:, lanes] = (bare - screened + bare * polar * screened).astype(jnp.bfloat16)
    if last:
        wait_in_order(refs)


def per_device(g_less, g_great, coulomb, precond):
    e_dev, order = g_less.shape[1:]
    n_energy = lax.axis_size("energy")
    n_tile = lax.axis_size("tile")
    total = e_dev * n_energy
    chunk = -(-order // n_energy)
    vmem = pl.BlockSpec(memory_space=pltpu.VMEM)
    smem = pl.BlockSpec(memory_space=pltpu.SMEM)

    limit = pltpu.CompilerParams(vmem_limit_bytes=VMEM_BYTES)
    matrices = [high_low(m) for m in dft_matrices(total)]
    forward = jnp.asarray(np.stack([np.concatenate(pair, axis=1) for pair in matrices]))
    backward = jnp.asarray(np.stack([np.ascontiguousarray(high.T) for high, _ in matrices]))

    hbm = pl.BlockSpec(memory_space=pltpu.HBM)
    g_less, g_great, forward, backward = (
        pltpu.with_memory_space_constraint(x, pltpu.HBM) for x in (g_less, g_great, forward, backward)
    )
    pieces, forward, backward = pl.pallas_call(
        lambda *refs: pack_kernel(chunk, *refs),
        out_shape=(
            jax.ShapeDtypeStruct((n_energy, 24, LANES), jnp.bfloat16),
            jax.ShapeDtypeStruct(forward.shape, jnp.bfloat16),
            jax.ShapeDtypeStruct(backward.shape, jnp.bfloat16),
        ),
        in_specs=[hbm] * 4,
        out_specs=(vmem,) * 3,
        scratch_shapes=[pltpu.VMEM(g_less.shape, jnp.bfloat16)] * 2 + [pltpu.SemaphoreType.DMA((4,))],
        compiler_params=limit,
    )(g_less, g_great, forward, backward)
    pieces = lax.all_to_all(pieces, "energy", 0, 0, tiled=True)
    scale = 0.25 / math.sqrt(total) * 2.0 / (2 * total)
    lags = pl.pallas_call(
        lambda *refs: correlate_kernel(chunk, scale, *refs),
        out_shape=jax.ShapeDtypeStruct((n_energy, 8, LANES), jnp.bfloat16),
        in_specs=[vmem] * 3,
        out_specs=vmem,
        compiler_params=limit,
    )(pieces, forward, backward)
    lags = lax.all_to_all(lags, "energy", 0, 0, tiled=True)
    bare = coulomb[None, :]
    plane = jax.ShapeDtypeStruct((e_dev, order), jnp.float32)
    plane_b = jax.ShapeDtypeStruct((e_dev, order), jnp.bfloat16)
    in_order = [
        pltpu.VMEM((order // LANES, e_dev, LANES), jnp.float32),
        pltpu.SemaphoreType.DMA((order // LANES,)),
    ]
    polar_sorted, resid_b = pl.pallas_call(
        lambda *refs: unpack_kernel(chunk, *refs),
        out_shape=(plane, plane_b),
        in_specs=[vmem] * 2,
        out_specs=(vmem,) * 2,
        compiler_params=limit,
    )(lags, bare)
    polar = pl.pallas_call(
        order_kernel,
        out_shape=plane,
        in_specs=[vmem],
        out_specs=hbm,
        scratch_shapes=in_order,
        compiler_params=limit,
        cost_estimate=pl.CostEstimate(flops=1000, bytes_accessed=1000, transcendentals=0),
    )(polar_sorted)
    parity = (lax.axis_index("tile") % 2).astype(jnp.int32).reshape(1)
    screened = polar_sorted
    chip_pairs = [(i, i ^ 1) for i in range(n_tile)]
    far_pairs = [(i, i + 1 if i % 2 else i - 1) for i in range(1, n_tile - 1)]
    for step in range(ITERS):
        last = step == ITERS - 1
        far = lax.ppermute(resid_b, "tile", far_pairs)
        chip = lax.ppermute(resid_b, "tile", chip_pairs)
        near = pl.pallas_call(
            near_kernel,
            out_shape=plane,
            in_specs=[smem] + [vmem] * 3,
            out_specs=vmem,
            compiler_params=limit,
        )(parity, resid_b, chip, precond)
        out = pl.pallas_call(
            lambda *refs, last=last: step_kernel(last, *refs),
            out_shape=(plane,) if last else (plane, plane_b),
            in_specs=[smem] + [vmem] * 6,
            out_specs=(hbm,) if last else (vmem, vmem),
            scratch_shapes=in_order if last else [],
            compiler_params=limit,
        )(parity, near, far, polar_sorted, screened, bare, precond)
        screened = out[0]
        resid_b = out[-1]
    return (polar, screened)


def solution(mesh):
    placed = (
        P(None, "energy", "tile"),
        P(None, "energy", "tile"),
        P("tile"),
        P(None, "tile", None),
    )
    return jax.shard_map(
        per_device,
        mesh=mesh,
        in_specs=placed,
        out_specs=(P("energy", "tile"), P("energy", "tile")),
        check_vma=False,
    )
```

```python
import math

import jax
import jax.numpy as jnp
import ml_dtypes
import numpy as np
from jax import lax
from jax.experimental import pallas as pl
from jax.experimental.pallas import tpu as pltpu
from jax.sharding import PartitionSpec as P

EARLY = 4
LANES = 128
VMEM_BYTES = 16 * 1024 * 1024
SLOT = 32


def dft_matrices(total):
    rows, length = total // 4, 2 * total
    freq = np.arange(rows)[:, None]
    matrices = []
    for r in range(4):
        turn = (freq * (4 * np.arange(rows)[None, :] + r)) % length
        cos, sin = np.cos(2.0 * np.pi * turn / length), np.sin(2.0 * np.pi * turn / length)
        sin[0] = 1.0 - 2.0 * (np.arange(rows) % 2)
        matrices.append(np.concatenate([cos, sin], axis=0))
    return matrices


def high_low(matrix):
    exact = matrix.astype(np.float32)
    high = exact.astype(ml_dtypes.bfloat16)
    low = (exact - high.astype(np.float32)).astype(ml_dtypes.bfloat16)
    return high, low


def pack_kernel(chunk, less_hbm, great_hbm, fwd_hbm, back_hbm, out_ref, fwd_ref, back_ref, less_ref, great_ref, sems):
    copies = [
        pltpu.make_async_copy(src, dst, sems.at[n])
        for n, (src, dst) in enumerate(
            ((less_hbm, less_ref), (great_hbm, great_ref), (fwd_hbm, fwd_ref), (back_hbm, back_ref))
        )
    ]
    for copy in copies:
        copy.start()
    e_dev, order = less_ref.shape[1], less_ref.shape[2]
    row = lax.broadcasted_iota(jnp.int32, (4 * e_dev, 4 * e_dev), 0)
    col = lax.broadcasted_iota(jnp.int32, (4 * e_dev, 4 * e_dev), 1)
    inner = row % e_dev
    source = row - inner + 4 * (inner % 8) + inner // 8
    select = jnp.where(col == source, 1.0, 0.0).astype(jnp.bfloat16)
    lane = lax.broadcasted_iota(jnp.int32, (e_dev, LANES), 1)
    in_slot = lax.broadcasted_iota(jnp.int32, (8, LANES), 1) % SLOT
    spare = SLOT - chunk
    copies[0].wait()
    copies[1].wait()
    rows = jnp.concatenate([less_ref[0], less_ref[1], great_ref[0], great_ref[1]], axis=0)
    sorted_rows = jnp.dot(select, rows, preferred_element_type=jnp.float32)
    for p in range(out_ref.shape[0]):
        low = chunk * p
        high = min(low + chunk, order) - 1
        first, last = low // LANES, high // LANES
        piece = None
        for q in range(4):
            shift = (SLOT * q - low) % LANES
            part = sorted_rows[e_dev * q : e_dev * (q + 1)]
            moved = pltpu.roll(part[:, LANES * first : LANES * (first + 1)], shift, 1)
            if last > first:
                after = pltpu.roll(part[:, LANES * last : LANES * (last + 1)], shift, 1)
                moved = jnp.where(lane >= SLOT * q + LANES * last - low, after, moved)
            piece = moved if q == 0 else jnp.where(lane >= SLOT * q, moved, piece)
        rest = piece[24:]
        full = [
            jnp.where(in_slot < chunk, piece[8 * g : 8 * (g + 1)], pltpu.roll(rest, chunk - spare * g, 1))
            for g in range(3)
        ]
        out_ref[p] = jnp.concatenate(full, axis=0).astype(jnp.bfloat16)
    copies[2].wait()
    copies[3].wait()


def product(a, b):
    return a[0] * b[0] + a[1] * b[1], a[1] * b[0] - a[0] * b[1]


def correlate_kernel(chunk, scale, data_ref, fwd_ref, back_ref, out_ref):
    blocks = data_ref.shape[0]
    rows = back_ref.shape[1]
    in_slot = lax.broadcasted_iota(jnp.int32, (blocks, 8, LANES), 2) % SLOT
    spare = SLOT - chunk
    packed = [data_ref[:, 8 * g : 8 * (g + 1), :].astype(jnp.float32) for g in range(3)]
    rest = None
    for g in range(3):
        moved = pltpu.roll(packed[g], LANES - chunk + spare * g, 2)
        rest = moved if g == 0 else jnp.where(in_slot >= spare * g, moved, rest)
    c, s = [], []
    for r in range(4):
        energies = (packed + [rest])[r].reshape(rows, LANES).astype(jnp.bfloat16)
        full = jnp.dot(fwd_ref[r, :, :rows], energies, preferred_element_type=jnp.float32)
        full = full + jnp.dot(fwd_ref[r, :, rows:], energies, preferred_element_type=jnp.float32)
        c.append(full[:rows])
        s.append(full[rows:])

    def times_other(spectrum):
        return product(spectrum, [pltpu.roll(x, LANES // 2, 1) for x in spectrum])

    c02, c02m, c13, c13m = c[0] + c[2], c[0] - c[2], c[1] + c[3], c[1] - c[3]
    s02, s02m, s13, s13m = s[0] + s[2], s[0] - s[2], s[1] + s[3], s[1] - s[3]
    low, low_i = times_other((c02 + c13, s02 + s13))
    top, top_i = times_other((c02 - c13, s13 - s02))
    under, under_i = times_other((c02m + s13m, c13m - s02m))
    over, over_i = times_other((c02m - s13m, c13m + s02m))
    pairs = (
        (low + top + under + over, low_i - top_i - under_i + over_i),
        (low - top + under_i + over_i, low_i + top_i + under - over),
        (low + top - under - over, low_i - top_i + under_i - over_i),
        (low - top - under_i - over_i, low_i + top_i - under + over),
    )
    root = math.sqrt(0.5)
    c0, z0 = [x[:8] for x in c], [x[:8] for x in s]
    zero = jnp.zeros_like(c0[0])
    first, _ = times_other((c0[0] + c0[1] + c0[2] + c0[3], zero))
    final, _ = times_other((c0[0] - c0[1] + c0[2] - c0[3], zero))
    mid, mid_i = times_other((c0[0] - c0[2], c0[1] - c0[3]))
    turned_sum, turned_dif = root * (z0[1] + z0[3]), root * (z0[1] - z0[3])
    quarter, quarter_i = times_other((z0[0] + turned_dif, turned_sum + z0[2]))
    three, three_i = times_other((z0[0] - turned_dif, turned_sum - z0[2]))
    edges = (
        (0.5 * (first + final) + mid, quarter + three),
        (0.5 * (first - final) + mid_i, root * (quarter - three + quarter_i + three_i)),
        (0.5 * (first + final) - mid, quarter_i - three_i),
        (0.5 * (first - final) - mid_i, root * (three - quarter + quarter_i + three_i)),
    )
    edge = lax.broadcasted_iota(jnp.int32, (8, LANES), 0) == 0
    lane = lax.broadcasted_iota(jnp.int32, (blocks, 8, LANES), 2)
    result = None
    for r in range(4):
        both = []
        for value, at_edge in zip(pairs[r], edges[r]):
            value = jnp.concatenate([jnp.where(edge, at_edge, value[:8]), value[8:]], axis=0)
            both.append(value - pltpu.roll(value, LANES - SLOT, 1))
        both = jnp.concatenate(both, axis=0).astype(jnp.bfloat16)
        lags = jnp.dot(back_ref[r], both, preferred_element_type=jnp.float32) * scale
        lags = lags.reshape(blocks, 8, LANES)
        result = lags if r == 0 else jnp.where(lane >= SLOT * r, pltpu.roll(lags, SLOT * r, 2), result)
    out_ref[...] = result.astype(out_ref.dtype)


def tile_copy(refs, tile):
    out_hbm, order_ref, sems = refs
    return pltpu.make_async_copy(
        order_ref.at[tile], out_hbm.at[:, LANES * tile : LANES * (tile + 1)], sems.at[tile]
    )


def store_in_order(sorted_rows, refs, at):
    for n in range(sorted_rows.shape[1] // LANES):
        lanes = slice(LANES * n, LANES * (n + 1))
        tile = at // LANES + n
        for r in range(4):
            refs[1][tile, pl.ds(r, 8, stride=4), :] = sorted_rows[8 * r : 8 * (r + 1), lanes]
        tile_copy(refs, tile).start()


def wait_in_order(refs):
    for tile in range(refs[1].shape[0]):
        tile_copy(refs, tile).wait()


def unpack_kernel(chunk, data_ref, bare_ref, sorted_ref, message_ref):
    e_dev, order = sorted_ref.shape
    lane = lax.broadcasted_iota(jnp.int32, (8, LANES), 1)
    for g in range(4):
        for tile in range(order // LANES):
            value = None
            p = (LANES * tile) // chunk
            while p < data_ref.shape[0] and chunk * p < LANES * (tile + 1):
                begin = chunk * p - LANES * tile
                moved = pltpu.roll(data_ref[p].astype(jnp.float32), (begin - SLOT * g) % LANES, 1)
                value = moved if value is None else jnp.where(lane >= begin, moved, value)
                p += 1
            sorted_ref[8 * g : 8 * (g + 1), LANES * tile : LANES * (tile + 1)] = value
    message_ref[:e_dev] = sorted_ref[...].astype(jnp.bfloat16)
    row = lax.broadcasted_iota(jnp.int32, (8, order), 0)
    rest, lines = bare_ref[...], jnp.zeros((8, order), jnp.float32)
    for n in range(3):
        part = rest.astype(jnp.bfloat16).astype(jnp.float32)
        lines = jnp.where(row == n, part, lines)
        rest = rest - part
    message_ref[e_dev:] = lines.astype(jnp.bfloat16)


def opened(message_ref):
    e_dev = message_ref.shape[0] - 8
    polar = message_ref[:e_dev].astype(jnp.float32)
    lines = message_ref[e_dev:].astype(jnp.float32)
    bare = lines[0:1] + lines[1:2] + lines[2:3]
    return polar, bare, bare * polar * bare


def updated(polar, bare, resid, total):
    corr = total.astype(jnp.bfloat16).astype(jnp.float32)
    screened = bare + 0.5 * resid + corr
    return screened, (bare - screened + bare * polar * screened).astype(jnp.bfloat16)


def order_kernel(sorted_ref, *refs):
    store_in_order(sorted_ref[...], refs, 0)
    wait_in_order(refs)


def times(rows, tile):
    return jnp.dot(rows, tile, preferred_element_type=jnp.float32)


def near_kernel(first, place_ref, own_ref, chip_ref, precond_ref, out_ref):
    own, chip = (opened(x)[2].astype(jnp.bfloat16) if first else x[...] for x in (own_ref, chip_ref))
    out_ref[...] = times(own, precond_ref[0]) + times(chip, precond_ref[2 - place_ref[0] % 2])


def first_kernel(place_ref, near_ref, own_ref, far_ref, behind_ref, precond_ref, far_precond_ref, screened_ref, next_ref, far_next_ref):
    odd = place_ref[0] % 2
    polar, bare, resid = opened(own_ref)
    far_polar, far_bare, far_resid = opened(far_ref)
    behind = opened(behind_ref)[2].astype(jnp.bfloat16)
    own, far = resid.astype(jnp.bfloat16), far_resid.astype(jnp.bfloat16)
    total = near_ref[...] + times(far, precond_ref[1 + odd])
    screened_ref[...], next_ref[...] = updated(polar, bare, resid, total)
    total = times(far, far_precond_ref[0]) + times(behind, far_precond_ref[1 + odd]) + times(own, far_precond_ref[2 - odd])
    far_next_ref[...] = updated(far_polar, far_bare, far_resid, total)[1]


def last_kernel(place_ref, near_ref, far_ref, far_next_ref, polar_ref, screened_ref, bare_ref, precond_ref, *refs):
    which = 1 + place_ref[0] % 2
    far = jnp.where(place_ref[0] >= 2, far_next_ref[...], far_ref[...])
    width = 256
    for at in range(0, far.shape[1], width):
        lanes = slice(at, at + width)
        bare, polar, screened = bare_ref[:, lanes], polar_ref[:, lanes], screened_ref[:, lanes]
        resid = bare - screened + bare * polar * screened
        total = near_ref[:, lanes] + times(far, precond_ref[which, :, lanes])
        corr = total.astype(jnp.bfloat16).astype(jnp.float32)
        store_in_order(screened + 0.5 * resid + corr, refs, at)
    wait_in_order(refs)


def pack_call(chunk, n_energy, limit, g_less, g_great, forward, backward):
    vmem = pl.BlockSpec(memory_space=pltpu.VMEM)
    hbm = pl.BlockSpec(memory_space=pltpu.HBM)
    return pl.pallas_call(
        lambda *refs: pack_kernel(chunk, *refs),
        out_shape=(
            jax.ShapeDtypeStruct((n_energy, 24, LANES), jnp.bfloat16),
            jax.ShapeDtypeStruct(forward.shape, jnp.bfloat16),
            jax.ShapeDtypeStruct(backward.shape, jnp.bfloat16),
        ),
        in_specs=[hbm] * 4,
        out_specs=(vmem,) * 3,
        scratch_shapes=[pltpu.VMEM(g_less.shape, jnp.bfloat16)] * 2 + [pltpu.SemaphoreType.DMA((4,))],
        compiler_params=limit,
    )(g_less, g_great, forward, backward)


def per_device(g_less, g_great, coulomb, precond):
    e_dev, order = g_less.shape[1:]
    n_energy = lax.axis_size("energy")
    n_tile = lax.axis_size("tile")
    total = e_dev * n_energy
    chunk = -(-order // n_energy)
    vmem = pl.BlockSpec(memory_space=pltpu.VMEM)
    smem = pl.BlockSpec(memory_space=pltpu.SMEM)

    limit = pltpu.CompilerParams(vmem_limit_bytes=VMEM_BYTES)
    matrices = [high_low(m) for m in dft_matrices(total)]
    forward = jnp.asarray(np.stack([np.concatenate(pair, axis=1) for pair in matrices]))
    backward = jnp.asarray(np.stack([np.ascontiguousarray(high.T) for high, _ in matrices]))

    hbm = pl.BlockSpec(memory_space=pltpu.HBM)
    g_less, g_great, forward, backward = (
        pltpu.with_memory_space_constraint(x, pltpu.HBM) for x in (g_less, g_great, forward, backward)
    )
    block = [(i, i + 1 if i % 2 else i - 1) for i in range(1, n_tile - 1)]
    ahead = [(i, i + 2 if i % 2 == 0 else i - 2) for i in range(n_tile) if 0 <= (i + 2 if i % 2 == 0 else i - 2) < n_tile]
    early = [e % (n_energy // 2) < EARLY for e in range(n_energy)]

    def pairs_of(pairs, chosen):
        return [(e * n_tile + i, e * n_tile + j) for e in range(n_energy) if chosen[e] for i, j in pairs]

    far_precond = lax.ppermute(precond, ("energy", "tile"), pairs_of(block, early))
    pieces, forward, backward = pack_call(
        chunk, n_energy, limit, g_less, g_great, forward, backward
    )
    pieces = lax.all_to_all(pieces, "energy", 0, 0, tiled=True)
    scale = 0.25 / math.sqrt(total) * 2.0 / (2 * total)
    lags = pl.pallas_call(
        lambda *refs: correlate_kernel(chunk, scale, *refs),
        out_shape=jax.ShapeDtypeStruct((n_energy, 8, LANES), jnp.bfloat16),
        in_specs=[vmem] * 3,
        out_specs=vmem,
        compiler_params=limit,
    )(pieces, forward, backward)
    lags = lax.all_to_all(lags, "energy", 0, 0, tiled=True)
    bare = coulomb[None, :]
    plane = jax.ShapeDtypeStruct((e_dev, order), jnp.float32)
    plane_b = jax.ShapeDtypeStruct((e_dev, order), jnp.bfloat16)
    in_order = [
        pltpu.VMEM((order // LANES, e_dev, LANES), jnp.float32),
        pltpu.SemaphoreType.DMA((order // LANES,)),
    ]
    polar_sorted, message = pl.pallas_call(
        lambda *refs: unpack_kernel(chunk, *refs),
        out_shape=(plane, jax.ShapeDtypeStruct((e_dev + 8, order), jnp.bfloat16)),
        in_specs=[vmem] * 2,
        out_specs=(vmem,) * 2,
        compiler_params=limit,
    )(lags, bare)
    polar = pl.pallas_call(
        order_kernel,
        out_shape=plane,
        in_specs=[vmem],
        out_specs=hbm,
        scratch_shapes=in_order,
        compiler_params=limit,
        cost_estimate=pl.CostEstimate(flops=1000, bytes_accessed=1000, transcendentals=0),
    )(polar_sorted)
    is_early = (lax.axis_index("energy") % (n_energy // 2) < EARLY).astype(jnp.int32)
    place = (lax.axis_index("tile") % 2 + 2 * is_early).astype(jnp.int32).reshape(1)
    chip_pairs = [(i, i ^ 1) for i in range(n_tile)]

    def near_call(first, own, chip):
        return pl.pallas_call(
            lambda *refs: near_kernel(first, *refs),
            out_shape=plane,
            in_specs=[smem] + [vmem] * 3,
            out_specs=vmem,
            compiler_params=limit,
        )(place, own, chip, precond)

    behind = lax.ppermute(message, ("energy", "tile"), pairs_of(ahead, early))
    far = lax.ppermute(message, "tile", block)
    chip = lax.ppermute(message, "tile", chip_pairs)
    near = near_call(True, message, chip)
    screened, resid_b, far_b = pl.pallas_call(
        first_kernel,
        out_shape=(plane, plane_b, plane_b),
        in_specs=[smem] + [vmem] * 6,
        out_specs=(vmem,) * 3,
        compiler_params=limit,
    )(place, near, message, far, behind, precond, far_precond)
    far = lax.ppermute(resid_b, ("energy", "tile"), pairs_of(block, [not e for e in early]))
    chip = lax.ppermute(resid_b, "tile", chip_pairs)
    near = near_call(False, resid_b, chip)
    screened = pl.pallas_call(
        last_kernel,
        out_shape=plane,
        in_specs=[smem] + [vmem] * 7,
        out_specs=hbm,
        scratch_shapes=in_order,
        compiler_params=limit,
    )(place, near, far, far_b, polar_sorted, screened, bare, precond)
    return (polar, screened)


def solution(mesh):
    placed = (
        P(None, "energy", "tile"),
        P(None, "energy", "tile"),
        P("tile"),
        P(None, "tile", None),
    )
    return jax.shard_map(
        per_device,
        mesh=mesh,
        in_specs=placed,
        out_specs=(P("energy", "tile"), P("energy", "tile")),
        check_vma=False,
    )
```

```python
import math

import jax
import jax.numpy as jnp
import ml_dtypes
import numpy as np
from jax import lax
from jax.experimental import pallas as pl
from jax.experimental.pallas import tpu as pltpu
from jax.sharding import PartitionSpec as P

ITERS = 2
LANES = 128
VMEM_BYTES = 16 * 1024 * 1024
SLOT = 32


def dft_matrices(total):
    rows, length = total // 4, 2 * total
    freq = np.arange(rows)[:, None]
    matrices = []
    for r in range(4):
        turn = (freq * (4 * np.arange(rows)[None, :] + r)) % length
        cos, sin = np.cos(2.0 * np.pi * turn / length), np.sin(2.0 * np.pi * turn / length)
        sin[0] = 1.0 - 2.0 * (np.arange(rows) % 2)
        matrices.append(np.concatenate([cos, sin], axis=0))
    return matrices


def high_low(matrix):
    exact = matrix.astype(np.float32)
    high = exact.astype(ml_dtypes.bfloat16)
    low = (exact - high.astype(np.float32)).astype(ml_dtypes.bfloat16)
    return high, low


def pack_kernel(chunk, less_hbm, great_hbm, fwd_hbm, back_hbm, out_ref, fwd_ref, back_ref, less_ref, great_ref, sems):
    copies = [
        pltpu.make_async_copy(src, dst, sems.at[n])
        for n, (src, dst) in enumerate(
            ((less_hbm, less_ref), (great_hbm, great_ref), (fwd_hbm, fwd_ref), (back_hbm, back_ref))
        )
    ]
    for copy in copies:
        copy.start()
    e_dev, order = less_ref.shape[1], less_ref.shape[2]
    row = lax.broadcasted_iota(jnp.int32, (4 * e_dev, 4 * e_dev), 0)
    col = lax.broadcasted_iota(jnp.int32, (4 * e_dev, 4 * e_dev), 1)
    inner = row % e_dev
    source = row - inner + 4 * (inner % 8) + inner // 8
    select = jnp.where(col == source, 1.0, 0.0).astype(jnp.bfloat16)
    lane = lax.broadcasted_iota(jnp.int32, (8, LANES), 1)
    spare = SLOT - chunk
    copies[0].wait()
    copies[1].wait()
    rows = jnp.concatenate([less_ref[0], less_ref[1], great_ref[0], great_ref[1]], axis=0)
    sorted_rows = jnp.dot(select, rows, preferred_element_type=jnp.float32)

    def moved(q, r, tile, shift):
        part = sorted_rows[e_dev * q + 8 * r : e_dev * q + 8 * (r + 1), LANES * tile : LANES * (tile + 1)]
        return pltpu.roll(part, shift % LANES, 1) if shift % LANES else part

    tiles = range(order // LANES)
    main = [[[moved(q, g, t, SLOT * q) for t in tiles] for g in range(3)] for q in range(4)]
    rest = [[[moved(q, 3, t, SLOT * q + chunk - spare * g) for t in tiles] for g in range(3)] for q in range(4)]
    for p in range(out_ref.shape[0]):
        low = chunk * p
        first, last = low // LANES, (min(low + chunk, order) - 1) // LANES
        turn = low % LANES
        place = (lane - turn) & (LANES - 1)
        inner = place & (SLOT - 1)

        def chain(parts, g, tile):
            value = parts[0][g][tile]
            for q in range(1, 4):
                value = jnp.where(place >= SLOT * q, parts[q][g][tile], value)
            return value

        groups = []
        for g in range(3):
            ours, extra = chain(main, g, first), chain(rest, g, first)
            if last > first:
                ours = jnp.where(inner >= LANES - turn, chain(main, g, last), ours)
                extra = jnp.where(inner - chunk + spare * g >= LANES - turn, chain(rest, g, last), extra)
            groups.append(jnp.where(inner < chunk, ours, extra))
        out_ref[p] = jnp.concatenate(groups, axis=0).astype(jnp.bfloat16)
    copies[2].wait()
    copies[3].wait()


def product(a, b):
    return a[0] * b[0] + a[1] * b[1], a[1] * b[0] - a[0] * b[1]


def correlate_kernel(chunk, scale, data_ref, fwd_ref, back_ref, out_ref):
    blocks = data_ref.shape[0]
    rows = back_ref.shape[1]
    turn = chunk * lax.axis_index("energy")
    place = (lax.broadcasted_iota(jnp.int32, (blocks, 8, LANES), 2) - turn) & (LANES - 1)
    in_slot = place & (SLOT - 1)
    spare = SLOT - chunk
    packed = [data_ref[:, 8 * g : 8 * (g + 1), :].astype(jnp.float32) for g in range(3)]
    rest = None
    for g in range(3):
        moved = pltpu.roll(packed[g], LANES - chunk + spare * g, 2)
        rest = moved if g == 0 else jnp.where(in_slot >= spare * g, moved, rest)
    c, s = [], []
    for r in range(4):
        energies = (packed + [rest])[r].reshape(rows, LANES).astype(jnp.bfloat16)
        full = jnp.dot(fwd_ref[r, :, :rows], energies, preferred_element_type=jnp.float32)
        c.append(full[:rows])
        s.append(full[rows:])

    def times_other(spectrum):
        return product(spectrum, [pltpu.roll(x, LANES // 2, 1) for x in spectrum])

    c02, c02m, c13, c13m = c[0] + c[2], c[0] - c[2], c[1] + c[3], c[1] - c[3]
    s02, s02m, s13, s13m = s[0] + s[2], s[0] - s[2], s[1] + s[3], s[1] - s[3]
    low, low_i = times_other((c02 + c13, s02 + s13))
    top, top_i = times_other((c02 - c13, s13 - s02))
    under, under_i = times_other((c02m + s13m, c13m - s02m))
    over, over_i = times_other((c02m - s13m, c13m + s02m))
    pairs = (
        (low + top + under + over, low_i - top_i - under_i + over_i),
        (low - top + under_i + over_i, low_i + top_i + under - over),
        (low + top - under - over, low_i - top_i + under_i - over_i),
        (low - top - under_i - over_i, low_i + top_i - under + over),
    )
    root = math.sqrt(0.5)
    c0, z0 = [x[:8] for x in c], [x[:8] for x in s]
    zero = jnp.zeros_like(c0[0])
    first, _ = times_other((c0[0] + c0[1] + c0[2] + c0[3], zero))
    final, _ = times_other((c0[0] - c0[1] + c0[2] - c0[3], zero))
    mid, mid_i = times_other((c0[0] - c0[2], c0[1] - c0[3]))
    turned_sum, turned_dif = root * (z0[1] + z0[3]), root * (z0[1] - z0[3])
    quarter, quarter_i = times_other((z0[0] + turned_dif, turned_sum + z0[2]))
    three, three_i = times_other((z0[0] - turned_dif, turned_sum - z0[2]))
    edges = (
        (0.5 * (first + final) + mid, quarter + three),
        (0.5 * (first - final) + mid_i, root * (quarter - three + quarter_i + three_i)),
        (0.5 * (first + final) - mid, quarter_i - three_i),
        (0.5 * (first - final) - mid_i, root * (three - quarter + quarter_i + three_i)),
    )
    edge = lax.broadcasted_iota(jnp.int32, (8, LANES), 0) == 0
    result = None
    for r in range(4):
        both = []
        for value, at_edge in zip(pairs[r], edges[r]):
            value = jnp.concatenate([jnp.where(edge, at_edge, value[:8]), value[8:]], axis=0)
            both.append(value - pltpu.roll(value, LANES - SLOT, 1))
        both = jnp.concatenate(both, axis=0).astype(jnp.bfloat16)
        lags = jnp.dot(back_ref[r], both, preferred_element_type=jnp.float32) * scale
        lags = lags.reshape(blocks, 8, LANES)
        result = lags if r == 0 else jnp.where(place >= SLOT * r, pltpu.roll(lags, SLOT * r, 2), result)
    out_ref[...] = result.astype(out_ref.dtype)


def tile_copy(refs, tile):
    out_hbm, order_ref, sems = refs
    return pltpu.make_async_copy(
        order_ref.at[tile], out_hbm.at[:, LANES * tile : LANES * (tile + 1)], sems.at[tile]
    )


def store_in_order(sorted_rows, refs, at):
    for n in range(sorted_rows.shape[1] // LANES):
        lanes = slice(LANES * n, LANES * (n + 1))
        tile = at // LANES + n
        for r in range(4):
            refs[1][tile, pl.ds(r, 8, stride=4), :] = sorted_rows[8 * r : 8 * (r + 1), lanes]
        tile_copy(refs, tile).start()


def wait_in_order(refs):
    for tile in range(refs[1].shape[0]):
        tile_copy(refs, tile).wait()


def unpack_kernel(chunk, data_ref, bare_ref, sorted_ref, resid_ref):
    order = sorted_ref.shape[1]
    lane = lax.broadcasted_iota(jnp.int32, (8, LANES), 1)
    for g in range(4):
        lags = [pltpu.roll(data_ref[p].astype(jnp.float32), (-SLOT * g) % LANES, 1) for p in range(data_ref.shape[0])]
        for tile in range(order // LANES):
            value = None
            p = (LANES * tile) // chunk
            while p < data_ref.shape[0] and chunk * p < LANES * (tile + 1):
                begin = chunk * p - LANES * tile
                value = lags[p] if value is None else jnp.where(lane >= begin, lags[p], value)
                p += 1
            sorted_ref[8 * g : 8 * (g + 1), LANES * tile : LANES * (tile + 1)] = value
    bare = bare_ref[...]
    resid_ref[...] = (bare * sorted_ref[...] * bare).astype(jnp.bfloat16)


def order_kernel(sorted_ref, *refs):
    store_in_order(sorted_ref[...], refs, 0)
    wait_in_order(refs)


def times(rows, tile):
    return jnp.dot(rows, tile, preferred_element_type=jnp.float32)


def near_kernel(
    first, parity_ref, own_ref, chip_ref, polar_ref, screened_ref, bare_ref, precond_ref, near_ref, base_ref
):
    near_ref[...] = times(own_ref[...], precond_ref[0]) + times(chip_ref[...], precond_ref[2 - parity_ref[0]])
    bare, polar = bare_ref[...], polar_ref[...]
    screened = jnp.broadcast_to(bare, polar.shape) if first else screened_ref[...]
    base_ref[...] = screened + 0.5 * (bare - screened + bare * polar * screened)


def step_kernel(last, parity_ref, near_ref, base_ref, far_ref, polar_ref, bare_ref, precond_ref, *refs):
    which = 1 + parity_ref[0]
    far = far_ref[...]
    width = 256 if last else far.shape[1]
    for at in range(0, far.shape[1], width):
        lanes = slice(at, at + width)
        total = near_ref[:, lanes] + times(far, precond_ref[which, :, lanes])
        screened = base_ref[:, lanes] + total.astype(jnp.bfloat16).astype(jnp.float32)
        if last:
            store_in_order(screened, refs, at)
        else:
            bare = bare_ref[...]
            refs[0][...] = screened
            refs[1][...] = (bare - screened + bare * polar_ref[...] * screened).astype(jnp.bfloat16)
    if last:
        wait_in_order(refs)


def per_device(g_less, g_great, coulomb, precond):
    e_dev, order = g_less.shape[1:]
    n_energy = lax.axis_size("energy")
    n_tile = lax.axis_size("tile")
    total = e_dev * n_energy
    chunk = -(-order // n_energy)
    vmem = pl.BlockSpec(memory_space=pltpu.VMEM)
    smem = pl.BlockSpec(memory_space=pltpu.SMEM)

    limit = pltpu.CompilerParams(vmem_limit_bytes=VMEM_BYTES)
    matrices = [high_low(m) for m in dft_matrices(total)]
    forward = jnp.asarray(np.stack([high for high, _ in matrices]))
    backward = jnp.asarray(np.stack([np.ascontiguousarray(high.T) for high, _ in matrices]))

    hbm = pl.BlockSpec(memory_space=pltpu.HBM)
    g_less, g_great, forward, backward = (
        pltpu.with_memory_space_constraint(x, pltpu.HBM) for x in (g_less, g_great, forward, backward)
    )
    pieces, forward, backward = pl.pallas_call(
        lambda *refs: pack_kernel(chunk, *refs),
        out_shape=(
            jax.ShapeDtypeStruct((n_energy, 24, LANES), jnp.bfloat16),
            jax.ShapeDtypeStruct(forward.shape, jnp.bfloat16),
            jax.ShapeDtypeStruct(backward.shape, jnp.bfloat16),
        ),
        in_specs=[hbm] * 4,
        out_specs=(vmem,) * 3,
        scratch_shapes=[pltpu.VMEM(g_less.shape, jnp.bfloat16)] * 2 + [pltpu.SemaphoreType.DMA((4,))],
        compiler_params=limit,
    )(g_less, g_great, forward, backward)
    pieces = lax.all_to_all(pieces, "energy", 0, 0, tiled=True)
    scale = 0.25 / math.sqrt(total) * 2.0 / (2 * total)
    lags = pl.pallas_call(
        lambda *refs: correlate_kernel(chunk, scale, *refs),
        out_shape=jax.ShapeDtypeStruct((n_energy, 8, LANES), jnp.bfloat16),
        in_specs=[vmem] * 3,
        out_specs=vmem,
        compiler_params=limit,
    )(pieces, forward, backward)
    lags = lax.all_to_all(lags, "energy", 0, 0, tiled=True)
    bare = coulomb[None, :]
    plane = jax.ShapeDtypeStruct((e_dev, order), jnp.float32)
    plane_b = jax.ShapeDtypeStruct((e_dev, order), jnp.bfloat16)
    in_order = [
        pltpu.VMEM((order // LANES, e_dev, LANES), jnp.float32),
        pltpu.SemaphoreType.DMA((order // LANES,)),
    ]
    polar_sorted, resid_b = pl.pallas_call(
        lambda *refs: unpack_kernel(chunk, *refs),
        out_shape=(plane, plane_b),
        in_specs=[vmem] * 2,
        out_specs=(vmem,) * 2,
        compiler_params=limit,
    )(lags, bare)
    polar = pl.pallas_call(
        order_kernel,
        out_shape=plane,
        in_specs=[vmem],
        out_specs=hbm,
        scratch_shapes=in_order,
        compiler_params=limit,
        cost_estimate=pl.CostEstimate(flops=1000, bytes_accessed=1000, transcendentals=0),
    )(polar_sorted)
    parity = (lax.axis_index("tile") % 2).astype(jnp.int32).reshape(1)
    screened = polar_sorted
    chip_pairs = [(i, i ^ 1) for i in range(n_tile)]
    far_pairs = [(i, i + 1 if i % 2 else i - 1) for i in range(1, n_tile - 1)]
    for step in range(ITERS):
        last = step == ITERS - 1
        far = lax.ppermute(resid_b, "tile", far_pairs)
        chip = lax.ppermute(resid_b, "tile", chip_pairs)
        near, base = pl.pallas_call(
            lambda *refs, first=step == 0: near_kernel(first, *refs),
            out_shape=(plane, plane),
            in_specs=[smem] + [vmem] * 6,
            out_specs=(vmem,) * 2,
            compiler_params=limit,
        )(parity, resid_b, chip, polar_sorted, screened, bare, precond)
        out = pl.pallas_call(
            lambda *refs, last=last: step_kernel(last, *refs),
            out_shape=(plane,) if last else (plane, plane_b),
            in_specs=[smem] + [vmem] * 6,
            out_specs=(hbm,) if last else (vmem, vmem),
            scratch_shapes=in_order if last else [],
            compiler_params=limit,
        )(parity, near, base, far, polar_sorted, bare, precond)
        screened = out[0]
        resid_b = out[-1]
    return (polar, screened)


def solution(mesh):
    placed = (
        P(None, "energy", "tile"),
        P(None, "energy", "tile"),
        P("tile"),
        P(None, "tile", None),
    )
    return jax.shard_map(
        per_device,
        mesh=mesh,
        in_specs=placed,
        out_specs=(P("energy", "tile"), P("energy", "tile")),
        check_vma=False,
    )
```

```python
import math

import jax
import jax.numpy as jnp
import ml_dtypes
import numpy as np
from jax import lax
from jax.experimental import pallas as pl
from jax.experimental.pallas import tpu as pltpu
from jax.sharding import PartitionSpec as P

ITERS = 2
LANES = 128
VMEM_BYTES = 16 * 1024 * 1024
SLOT = 32


def dft_matrices(total):
    rows, length = total // 4, 2 * total
    freq = np.arange(rows)[:, None]
    matrices = []
    for r in range(4):
        turn = (freq * (4 * np.arange(rows)[None, :] + r)) % length
        cos, sin = np.cos(2.0 * np.pi * turn / length), np.sin(2.0 * np.pi * turn / length)
        sin[0] = 1.0 - 2.0 * (np.arange(rows) % 2)
        matrices.append(np.concatenate([cos, sin], axis=0))
    return matrices


def high_low(matrix):
    exact = matrix.astype(np.float32)
    high = exact.astype(ml_dtypes.bfloat16)
    low = (exact - high.astype(np.float32)).astype(ml_dtypes.bfloat16)
    return high, low


def pack_kernel(chunk, less_hbm, great_hbm, fwd_hbm, back_hbm, out_ref, fwd_ref, back_ref, less_ref, great_ref, sems):
    copies = [
        pltpu.make_async_copy(src, dst, sems.at[n])
        for n, (src, dst) in enumerate(
            (
                (less_hbm.at[0], less_ref.at[0]),
                (less_hbm.at[1], less_ref.at[1]),
                (great_hbm.at[0], great_ref.at[0]),
                (great_hbm.at[1], great_ref.at[1]),
                (fwd_hbm, fwd_ref),
                (back_hbm, back_ref),
            )
        )
    ]
    for copy in copies:
        copy.start()
    e_dev, order = less_ref.shape[1], less_ref.shape[2]
    row = lax.broadcasted_iota(jnp.int32, (e_dev, e_dev), 0)
    col = lax.broadcasted_iota(jnp.int32, (e_dev, e_dev), 1)
    source = 4 * (row % 8) + row // 8
    select = jnp.where(col == source, 1.0, 0.0).astype(jnp.bfloat16)
    lane = lax.broadcasted_iota(jnp.int32, (8, LANES), 1)
    spare = SLOT - chunk

    def moved(q, r, tile, shift):
        part = ordered[q][8 * r : 8 * (r + 1), LANES * tile : LANES * (tile + 1)]
        return pltpu.roll(part, shift % LANES, 1) if shift % LANES else part

    tiles = range(order // LANES)
    ordered, main, rest = [], [], []
    for q, ref in enumerate((less_ref.at[0], less_ref.at[1], great_ref.at[0], great_ref.at[1])):
        copies[q].wait()
        ordered.append(jnp.dot(select, ref[...], preferred_element_type=jnp.float32))
        main.append([[moved(q, g, t, SLOT * q) for t in tiles] for g in range(3)])
        rest.append([[moved(q, 3, t, SLOT * q + chunk - spare * g) for t in tiles] for g in range(3)])
    for p in range(out_ref.shape[0]):
        low = chunk * p
        first, last = low // LANES, (min(low + chunk, order) - 1) // LANES
        turn = low % LANES
        place = (lane - turn) & (LANES - 1)
        inner = place & (SLOT - 1)

        def chain(parts, g, tile):
            value = parts[0][g][tile]
            for q in range(1, 4):
                value = jnp.where(place >= SLOT * q, parts[q][g][tile], value)
            return value

        groups = []
        for g in range(3):
            ours, extra = chain(main, g, first), chain(rest, g, first)
            if last > first:
                ours = jnp.where(inner >= LANES - turn, chain(main, g, last), ours)
                extra = jnp.where(inner - chunk + spare * g >= LANES - turn, chain(rest, g, last), extra)
            groups.append(jnp.where(inner < chunk, ours, extra))
        out_ref[p] = jnp.concatenate(groups, axis=0).astype(jnp.bfloat16)
    copies[4].wait()
    copies[5].wait()


def product(a, b):
    return a[0] * b[0] + a[1] * b[1], a[1] * b[0] - a[0] * b[1]


def correlate_kernel(chunk, scale, data_ref, fwd_ref, back_ref, out_ref):
    blocks = data_ref.shape[0]
    rows = back_ref.shape[1]
    turn = chunk * lax.axis_index("energy")
    place = (lax.broadcasted_iota(jnp.int32, (blocks, 8, LANES), 2) - turn) & (LANES - 1)
    in_slot = place & (SLOT - 1)
    spare = SLOT - chunk
    packed = [data_ref[:, 8 * g : 8 * (g + 1), :].astype(jnp.float32) for g in range(3)]
    rest = None
    for g in range(3):
        moved = pltpu.roll(packed[g], LANES - chunk + spare * g, 2)
        rest = moved if g == 0 else jnp.where(in_slot >= spare * g, moved, rest)
    c, s = [], []
    for r in range(4):
        energies = (packed + [rest])[r].reshape(rows, LANES).astype(jnp.bfloat16)
        full = jnp.dot(fwd_ref[r, :, :rows], energies, preferred_element_type=jnp.float32)
        c.append(full[:rows])
        s.append(full[rows:])

    def times_other(spectrum):
        return product(spectrum, [pltpu.roll(x, LANES // 2, 1) for x in spectrum])

    c02, c02m, c13, c13m = c[0] + c[2], c[0] - c[2], c[1] + c[3], c[1] - c[3]
    s02, s02m, s13, s13m = s[0] + s[2], s[0] - s[2], s[1] + s[3], s[1] - s[3]
    low, low_i = times_other((c02 + c13, s02 + s13))
    top, top_i = times_other((c02 - c13, s13 - s02))
    under, under_i = times_other((c02m + s13m, c13m - s02m))
    over, over_i = times_other((c02m - s13m, c13m + s02m))
    pairs = (
        (low + top + under + over, low_i - top_i - under_i + over_i),
        (low - top + under_i + over_i, low_i + top_i + under - over),
        (low + top - under - over, low_i - top_i + under_i - over_i),
        (low - top - under_i - over_i, low_i + top_i - under + over),
    )
    root = math.sqrt(0.5)
    c0, z0 = [x[:8] for x in c], [x[:8] for x in s]
    zero = jnp.zeros_like(c0[0])
    first, _ = times_other((c0[0] + c0[1] + c0[2] + c0[3], zero))
    final, _ = times_other((c0[0] - c0[1] + c0[2] - c0[3], zero))
    mid, mid_i = times_other((c0[0] - c0[2], c0[1] - c0[3]))
    turned_sum, turned_dif = root * (z0[1] + z0[3]), root * (z0[1] - z0[3])
    quarter, quarter_i = times_other((z0[0] + turned_dif, turned_sum + z0[2]))
    three, three_i = times_other((z0[0] - turned_dif, turned_sum - z0[2]))
    edges = (
        (0.5 * (first + final) + mid, quarter + three),
        (0.5 * (first - final) + mid_i, root * (quarter - three + quarter_i + three_i)),
        (0.5 * (first + final) - mid, quarter_i - three_i),
        (0.5 * (first - final) - mid_i, root * (three - quarter + quarter_i + three_i)),
    )
    edge = lax.broadcasted_iota(jnp.int32, (8, LANES), 0) == 0
    result = None
    for r in range(4):
        both = []
        for value, at_edge in zip(pairs[r], edges[r]):
            value = jnp.concatenate([jnp.where(edge, at_edge, value[:8]), value[8:]], axis=0)
            both.append(value - pltpu.roll(value, LANES - SLOT, 1))
        both = jnp.concatenate(both, axis=0).astype(jnp.bfloat16)
        lags = jnp.dot(back_ref[r], both, preferred_element_type=jnp.float32) * scale
        lags = lags.reshape(blocks, 8, LANES)
        result = lags if r == 0 else jnp.where(place >= SLOT * r, pltpu.roll(lags, SLOT * r, 2), result)
    out_ref[...] = result.astype(out_ref.dtype)


def tile_copy(refs, tile):
    out_hbm, order_ref, sems = refs
    return pltpu.make_async_copy(
        order_ref.at[tile], out_hbm.at[:, LANES * tile : LANES * (tile + 1)], sems.at[tile]
    )


def store_in_order(sorted_rows, refs, at):
    for n in range(sorted_rows.shape[1] // LANES):
        lanes = slice(LANES * n, LANES * (n + 1))
        tile = at // LANES + n
        for r in range(4):
            refs[1][tile, pl.ds(r, 8, stride=4), :] = sorted_rows[8 * r : 8 * (r + 1), lanes]
        tile_copy(refs, tile).start()


def wait_in_order(refs):
    for tile in range(refs[1].shape[0]):
        tile_copy(refs, tile).wait()


def unpack_kernel(chunk, data_ref, bare_ref, sorted_ref, resid_ref):
    order = sorted_ref.shape[1]
    lane = lax.broadcasted_iota(jnp.int32, (8, LANES), 1)
    for g in range(4):
        lags = [pltpu.roll(data_ref[p].astype(jnp.float32), (-SLOT * g) % LANES, 1) for p in range(data_ref.shape[0])]
        for tile in range(order // LANES):
            value = None
            p = (LANES * tile) // chunk
            while p < data_ref.shape[0] and chunk * p < LANES * (tile + 1):
                begin = chunk * p - LANES * tile
                value = lags[p] if value is None else jnp.where(lane >= begin, lags[p], value)
                p += 1
            sorted_ref[8 * g : 8 * (g + 1), LANES * tile : LANES * (tile + 1)] = value
    bare = bare_ref[...]
    resid_ref[...] = (bare * sorted_ref[...] * bare).astype(jnp.bfloat16)


def order_kernel(sorted_ref, *refs):
    store_in_order(sorted_ref[...], refs, 0)
    wait_in_order(refs)


def times(rows, tile):
    return jnp.dot(rows, tile, preferred_element_type=jnp.float32)


def near_kernel(
    first, parity_ref, own_ref, chip_ref, polar_ref, screened_ref, bare_ref, precond_ref, near_ref, base_ref
):
    near_ref[...] = times(own_ref[...], precond_ref[0]) + times(chip_ref[...], precond_ref[2 - parity_ref[0]])
    bare, polar = bare_ref[...], polar_ref[...]
    screened = jnp.broadcast_to(bare, polar.shape) if first else screened_ref[...]
    base_ref[...] = screened + 0.5 * (bare - screened + bare * polar * screened)


def step_kernel(last, parity_ref, near_ref, base_ref, far_ref, polar_ref, bare_ref, precond_ref, *refs):
    which = 1 + parity_ref[0]
    far = far_ref[...]
    width = 256 if last else far.shape[1]
    for at in range(0, far.shape[1], width):
        lanes = slice(at, at + width)
        total = near_ref[:, lanes] + times(far, precond_ref[which, :, lanes])
        screened = base_ref[:, lanes] + total.astype(jnp.bfloat16).astype(jnp.float32)
        if last:
            store_in_order(screened, refs, at)
        else:
            bare = bare_ref[...]
            refs[0][...] = screened
            refs[1][...] = (bare - screened + bare * polar_ref[...] * screened).astype(jnp.bfloat16)
    if last:
        wait_in_order(refs)


def per_device(g_less, g_great, coulomb, precond):
    e_dev, order = g_less.shape[1:]
    n_energy = lax.axis_size("energy")
    n_tile = lax.axis_size("tile")
    total = e_dev * n_energy
    chunk = -(-order // n_energy)
    vmem = pl.BlockSpec(memory_space=pltpu.VMEM)
    smem = pl.BlockSpec(memory_space=pltpu.SMEM)

    limit = pltpu.CompilerParams(vmem_limit_bytes=VMEM_BYTES)
    matrices = [high_low(m) for m in dft_matrices(total)]
    forward = jnp.asarray(np.stack([high for high, _ in matrices]))
    backward = jnp.asarray(np.stack([np.ascontiguousarray(high.T) for high, _ in matrices]))

    hbm = pl.BlockSpec(memory_space=pltpu.HBM)
    g_less, g_great, forward, backward = (
        pltpu.with_memory_space_constraint(x, pltpu.HBM) for x in (g_less, g_great, forward, backward)
    )
    pieces, forward, backward = pl.pallas_call(
        lambda *refs: pack_kernel(chunk, *refs),
        out_shape=(
            jax.ShapeDtypeStruct((n_energy, 24, LANES), jnp.bfloat16),
            jax.ShapeDtypeStruct(forward.shape, jnp.bfloat16),
            jax.ShapeDtypeStruct(backward.shape, jnp.bfloat16),
        ),
        in_specs=[hbm] * 4,
        out_specs=(vmem,) * 3,
        scratch_shapes=[pltpu.VMEM(g_less.shape, jnp.bfloat16)] * 2 + [pltpu.SemaphoreType.DMA((6,))],
        compiler_params=limit,
    )(g_less, g_great, forward, backward)
    pieces = lax.all_to_all(pieces, "energy", 0, 0, tiled=True)
    scale = 0.25 / math.sqrt(total) * 2.0 / (2 * total)
    lags = pl.pallas_call(
        lambda *refs: correlate_kernel(chunk, scale, *refs),
        out_shape=jax.ShapeDtypeStruct((n_energy, 8, LANES), jnp.bfloat16),
        in_specs=[vmem] * 3,
        out_specs=vmem,
        compiler_params=limit,
    )(pieces, forward, backward)
    lags = lax.all_to_all(lags, "energy", 0, 0, tiled=True)
    bare = coulomb[None, :]
    plane = jax.ShapeDtypeStruct((e_dev, order), jnp.float32)
    plane_b = jax.ShapeDtypeStruct((e_dev, order), jnp.bfloat16)
    in_order = [
        pltpu.VMEM((order // LANES, e_dev, LANES), jnp.float32),
        pltpu.SemaphoreType.DMA((order // LANES,)),
    ]
    polar_sorted, resid_b = pl.pallas_call(
        lambda *refs: unpack_kernel(chunk, *refs),
        out_shape=(plane, plane_b),
        in_specs=[vmem] * 2,
        out_specs=(vmem,) * 2,
        compiler_params=limit,
    )(lags, bare)
    polar = pl.pallas_call(
        order_kernel,
        out_shape=plane,
        in_specs=[vmem],
        out_specs=hbm,
        scratch_shapes=in_order,
        compiler_params=limit,
        cost_estimate=pl.CostEstimate(flops=1000, bytes_accessed=1000, transcendentals=0),
    )(polar_sorted)
    parity = (lax.axis_index("tile") % 2).astype(jnp.int32).reshape(1)
    screened = polar_sorted
    chip_pairs = [(i, i ^ 1) for i in range(n_tile)]
    far_pairs = [(i, i + 1 if i % 2 else i - 1) for i in range(1, n_tile - 1)]
    for step in range(ITERS):
        last = step == ITERS - 1
        far = lax.ppermute(resid_b, "tile", far_pairs)
        chip = lax.ppermute(resid_b, "tile", chip_pairs)
        near, base = pl.pallas_call(
            lambda *refs, first=step == 0: near_kernel(first, *refs),
            out_shape=(plane, plane),
            in_specs=[smem] + [vmem] * 6,
            out_specs=(vmem,) * 2,
            compiler_params=limit,
        )(parity, resid_b, chip, polar_sorted, screened, bare, precond)
        out = pl.pallas_call(
            lambda *refs, last=last: step_kernel(last, *refs),
            out_shape=(plane,) if last else (plane, plane_b),
            in_specs=[smem] + [vmem] * 6,
            out_specs=(hbm,) if last else (vmem, vmem),
            scratch_shapes=in_order if last else [],
            compiler_params=limit,
        )(parity, near, base, far, polar_sorted, bare, precond)
        screened = out[0]
        resid_b = out[-1]
    return (polar, screened)


def solution(mesh):
    placed = (
        P(None, "energy", "tile"),
        P(None, "energy", "tile"),
        P("tile"),
        P(None, "tile", None),
    )
    return jax.shard_map(
        per_device,
        mesh=mesh,
        in_specs=placed,
        out_specs=(P("energy", "tile"), P("energy", "tile")),
        check_vma=False,
    )
```

```python
import math

import jax
import jax.numpy as jnp
import ml_dtypes
import numpy as np
from jax import lax
from jax.experimental import pallas as pl
from jax.experimental.pallas import tpu as pltpu
from jax.sharding import PartitionSpec as P

ITERS = 2
LANES = 128
VMEM_BYTES = 16 * 1024 * 1024
SLOT = 32


def dft_matrices(total):
    rows, length = total // 4, 2 * total
    freq = np.arange(rows)[:, None]
    matrices = []
    for r in range(4):
        turn = (freq * (4 * np.arange(rows)[None, :] + r)) % length
        cos, sin = np.cos(2.0 * np.pi * turn / length), np.sin(2.0 * np.pi * turn / length)
        sin[0] = 1.0 - 2.0 * (np.arange(rows) % 2)
        matrices.append(np.concatenate([cos, sin], axis=0))
    return matrices


def high_low(matrix):
    exact = matrix.astype(np.float32)
    high = exact.astype(ml_dtypes.bfloat16)
    low = (exact - high.astype(np.float32)).astype(ml_dtypes.bfloat16)
    return high, low


def pack_kernel(chunk, less_hbm, great_hbm, fwd_hbm, back_hbm, out_ref, fwd_ref, back_ref, less_ref, great_ref, sems):
    copies = [
        pltpu.make_async_copy(src, dst, sems.at[n])
        for n, (src, dst) in enumerate(
            ((less_hbm, less_ref), (great_hbm, great_ref), (fwd_hbm, fwd_ref), (back_hbm, back_ref))
        )
    ]
    for copy in copies:
        copy.start()
    e_dev, order = less_ref.shape[1], less_ref.shape[2]
    row = lax.broadcasted_iota(jnp.int32, (4 * e_dev, 4 * e_dev), 0)
    col = lax.broadcasted_iota(jnp.int32, (4 * e_dev, 4 * e_dev), 1)
    inner = row % e_dev
    source = row - inner + 4 * (inner % 8) + inner // 8
    select = jnp.where(col == source, 1.0, 0.0).astype(jnp.bfloat16)
    lane = lax.broadcasted_iota(jnp.int32, (8, LANES), 1)
    spare = SLOT - chunk
    copies[0].wait()
    copies[1].wait()
    rows = jnp.concatenate([less_ref[0], less_ref[1], great_ref[0], great_ref[1]], axis=0)
    sorted_rows = jnp.dot(select, rows, preferred_element_type=jnp.float32)

    def moved(q, r, tile, shift):
        part = sorted_rows[e_dev * q + 8 * r : e_dev * q + 8 * (r + 1), LANES * tile : LANES * (tile + 1)]
        return pltpu.roll(part, shift % LANES, 1) if shift % LANES else part

    tiles = range(order // LANES)
    main = [[[moved(q, g, t, SLOT * q) for t in tiles] for g in range(3)] for q in range(4)]
    rest = [[[moved(q, 3, t, SLOT * q + chunk - spare * g) for t in tiles] for g in range(3)] for q in range(4)]
    for p in range(out_ref.shape[0]):
        low = chunk * p
        first, last = low // LANES, (min(low + chunk, order) - 1) // LANES
        turn = low % LANES
        place = (lane - turn) & (LANES - 1)
        inner = place & (SLOT - 1)

        def chain(parts, g, tile):
            value = parts[0][g][tile]
            for q in range(1, 4):
                value = jnp.where(place >= SLOT * q, parts[q][g][tile], value)
            return value

        groups = []
        for g in range(3):
            ours, extra = chain(main, g, first), chain(rest, g, first)
            if last > first:
                ours = jnp.where(inner >= LANES - turn, chain(main, g, last), ours)
                extra = jnp.where(inner - chunk + spare * g >= LANES - turn, chain(rest, g, last), extra)
            groups.append(jnp.where(inner < chunk, ours, extra))
        out_ref[p] = jnp.concatenate(groups, axis=0).astype(jnp.bfloat16)
    copies[2].wait()
    copies[3].wait()


def product(a, b):
    return a[0] * b[0] + a[1] * b[1], a[1] * b[0] - a[0] * b[1]


def correlate_kernel(chunk, scale, data_ref, fwd_ref, back_ref, out_ref):
    blocks = data_ref.shape[0]
    rows = back_ref.shape[1]
    turn = chunk * lax.axis_index("energy")
    place = (lax.broadcasted_iota(jnp.int32, (blocks, 8, LANES), 2) - turn) & (LANES - 1)
    in_slot = place & (SLOT - 1)
    spare = SLOT - chunk
    packed = [data_ref[:, 8 * g : 8 * (g + 1), :].astype(jnp.float32) for g in range(3)]
    rest = None
    for g in range(3):
        moved = pltpu.roll(packed[g], LANES - chunk + spare * g, 2)
        rest = moved if g == 0 else jnp.where(in_slot >= spare * g, moved, rest)
    c, s = [], []
    for r in range(4):
        energies = (packed + [rest])[r].reshape(rows, LANES).astype(jnp.bfloat16)
        full = jnp.dot(fwd_ref[r, :, :rows], energies, preferred_element_type=jnp.float32)
        c.append(full[:rows])
        s.append(full[rows:])

    def times_other(spectrum):
        return product(spectrum, [pltpu.roll(x, LANES // 2, 1) for x in spectrum])

    c02, c02m, c13, c13m = c[0] + c[2], c[0] - c[2], c[1] + c[3], c[1] - c[3]
    s02, s02m, s13, s13m = s[0] + s[2], s[0] - s[2], s[1] + s[3], s[1] - s[3]
    low, low_i = times_other((c02 + c13, s02 + s13))
    top, top_i = times_other((c02 - c13, s13 - s02))
    under, under_i = times_other((c02m + s13m, c13m - s02m))
    over, over_i = times_other((c02m - s13m, c13m + s02m))
    pairs = (
        (low + top + under + over, low_i - top_i - under_i + over_i),
        (low - top + under_i + over_i, low_i + top_i + under - over),
        (low + top - under - over, low_i - top_i + under_i - over_i),
        (low - top - under_i - over_i, low_i + top_i - under + over),
    )
    root = math.sqrt(0.5)
    c0, z0 = [x[:8] for x in c], [x[:8] for x in s]
    zero = jnp.zeros_like(c0[0])
    first, _ = times_other((c0[0] + c0[1] + c0[2] + c0[3], zero))
    final, _ = times_other((c0[0] - c0[1] + c0[2] - c0[3], zero))
    mid, mid_i = times_other((c0[0] - c0[2], c0[1] - c0[3]))
    turned_sum, turned_dif = root * (z0[1] + z0[3]), root * (z0[1] - z0[3])
    quarter, quarter_i = times_other((z0[0] + turned_dif, turned_sum + z0[2]))
    three, three_i = times_other((z0[0] - turned_dif, turned_sum - z0[2]))
    edges = (
        (0.5 * (first + final) + mid, quarter + three),
        (0.5 * (first - final) + mid_i, root * (quarter - three + quarter_i + three_i)),
        (0.5 * (first + final) - mid, quarter_i - three_i),
        (0.5 * (first - final) - mid_i, root * (three - quarter + quarter_i + three_i)),
    )
    edge = lax.broadcasted_iota(jnp.int32, (8, LANES), 0) == 0
    result = None
    for r in range(4):
        both = []
        for value, at_edge in zip(pairs[r], edges[r]):
            value = jnp.concatenate([jnp.where(edge, at_edge, value[:8]), value[8:]], axis=0)
            both.append(value - pltpu.roll(value, LANES - SLOT, 1))
        both = jnp.concatenate(both, axis=0).astype(jnp.bfloat16)
        lags = jnp.dot(back_ref[r], both, preferred_element_type=jnp.float32) * scale
        lags = lags.reshape(blocks, 8, LANES)
        result = lags if r == 0 else jnp.where(place >= SLOT * r, pltpu.roll(lags, SLOT * r, 2), result)
    out_ref[...] = result.astype(out_ref.dtype)


def tile_copy(refs, tile):
    out_hbm, order_ref, sems = refs
    return pltpu.make_async_copy(
        order_ref.at[tile], out_hbm.at[:, LANES * tile : LANES * (tile + 1)], sems.at[tile]
    )


def store_in_order(sorted_rows, refs, at):
    for n in range(sorted_rows.shape[1] // LANES):
        lanes = slice(LANES * n, LANES * (n + 1))
        tile = at // LANES + n
        for r in range(4):
            refs[1][tile, pl.ds(r, 8, stride=4), :] = sorted_rows[8 * r : 8 * (r + 1), lanes]
        tile_copy(refs, tile).start()


def wait_in_order(refs):
    for tile in range(refs[1].shape[0]):
        tile_copy(refs, tile).wait()


def unpack_kernel(chunk, data_ref, bare_ref, sorted_ref, resid_ref):
    order = sorted_ref.shape[1]
    lane = lax.broadcasted_iota(jnp.int32, (8, LANES), 1)
    bare = bare_ref[...]
    for half in range(2):
        lags = [
            [pltpu.roll(data_ref[p].astype(jnp.float32), (-SLOT * g) % LANES, 1) for p in range(data_ref.shape[0])]
            for g in (2 * half, 2 * half + 1)
        ]
        rows = slice(16 * half, 16 * (half + 1))
        for tile in range(order // LANES):
            lanes = slice(LANES * tile, LANES * (tile + 1))
            values = []
            for pieces in lags:
                value = None
                p = (LANES * tile) // chunk
                while p < data_ref.shape[0] and chunk * p < LANES * (tile + 1):
                    begin = chunk * p - LANES * tile
                    value = pieces[p] if value is None else jnp.where(lane >= begin, pieces[p], value)
                    p += 1
                values.append(value)
            value = jnp.concatenate(values, axis=0)
            sorted_ref[rows, lanes] = value
            resid_ref[rows, lanes] = (bare[:, lanes] * value * bare[:, lanes]).astype(jnp.bfloat16)


def order_kernel(sorted_ref, *refs):
    store_in_order(sorted_ref[...], refs, 0)
    wait_in_order(refs)


def times(rows, tile):
    return jnp.dot(rows, tile, preferred_element_type=jnp.float32)


def near_kernel(
    first, parity_ref, own_ref, chip_ref, polar_ref, screened_ref, bare_ref, precond_ref, near_ref, base_ref
):
    near_ref[...] = times(own_ref[...], precond_ref[0]) + times(chip_ref[...], precond_ref[2 - parity_ref[0]])
    bare, polar = bare_ref[...], polar_ref[...]
    screened = jnp.broadcast_to(bare, polar.shape) if first else screened_ref[...]
    base_ref[...] = screened + 0.5 * (bare - screened + bare * polar * screened)


def step_kernel(last, parity_ref, near_ref, base_ref, far_ref, polar_ref, bare_ref, precond_ref, *refs):
    which = 1 + parity_ref[0]
    far = far_ref[...]
    width = 256 if last else far.shape[1]
    for at in range(0, far.shape[1], width):
        lanes = slice(at, at + width)
        total = near_ref[:, lanes] + times(far, precond_ref[which, :, lanes])
        screened = base_ref[:, lanes] + total.astype(jnp.bfloat16).astype(jnp.float32)
        if last:
            store_in_order(screened, refs, at)
        else:
            bare = bare_ref[...]
            refs[0][...] = screened
            refs[1][...] = (bare - screened + bare * polar_ref[...] * screened).astype(jnp.bfloat16)
    if last:
        wait_in_order(refs)


def per_device(g_less, g_great, coulomb, precond):
    e_dev, order = g_less.shape[1:]
    n_energy = lax.axis_size("energy")
    n_tile = lax.axis_size("tile")
    total = e_dev * n_energy
    chunk = -(-order // n_energy)
    vmem = pl.BlockSpec(memory_space=pltpu.VMEM)
    smem = pl.BlockSpec(memory_space=pltpu.SMEM)

    limit = pltpu.CompilerParams(vmem_limit_bytes=VMEM_BYTES)
    matrices = [high_low(m) for m in dft_matrices(total)]
    forward = jnp.asarray(np.stack([high for high, _ in matrices]))
    backward = jnp.asarray(np.stack([np.ascontiguousarray(high.T) for high, _ in matrices]))

    hbm = pl.BlockSpec(memory_space=pltpu.HBM)
    g_less, g_great, forward, backward = (
        pltpu.with_memory_space_constraint(x, pltpu.HBM) for x in (g_less, g_great, forward, backward)
    )
    pieces, forward, backward = pl.pallas_call(
        lambda *refs: pack_kernel(chunk, *refs),
        out_shape=(
            jax.ShapeDtypeStruct((n_energy, 24, LANES), jnp.bfloat16),
            jax.ShapeDtypeStruct(forward.shape, jnp.bfloat16),
            jax.ShapeDtypeStruct(backward.shape, jnp.bfloat16),
        ),
        in_specs=[hbm] * 4,
        out_specs=(vmem,) * 3,
        scratch_shapes=[pltpu.VMEM(g_less.shape, jnp.bfloat16)] * 2 + [pltpu.SemaphoreType.DMA((4,))],
        compiler_params=limit,
    )(g_less, g_great, forward, backward)
    pieces = lax.all_to_all(pieces, "energy", 0, 0, tiled=True)
    scale = 0.25 / math.sqrt(total) * 2.0 / (2 * total)
    lags = pl.pallas_call(
        lambda *refs: correlate_kernel(chunk, scale, *refs),
        out_shape=jax.ShapeDtypeStruct((n_energy, 8, LANES), jnp.bfloat16),
        in_specs=[vmem] * 3,
        out_specs=vmem,
        compiler_params=limit,
    )(pieces, forward, backward)
    lags = lax.all_to_all(lags, "energy", 0, 0, tiled=True)
    bare = coulomb[None, :]
    plane = jax.ShapeDtypeStruct((e_dev, order), jnp.float32)
    plane_b = jax.ShapeDtypeStruct((e_dev, order), jnp.bfloat16)
    in_order = [
        pltpu.VMEM((order // LANES, e_dev, LANES), jnp.float32),
        pltpu.SemaphoreType.DMA((order // LANES,)),
    ]
    polar_sorted, resid_b = pl.pallas_call(
        lambda *refs: unpack_kernel(chunk, *refs),
        out_shape=(plane, plane_b),
        in_specs=[vmem] * 2,
        out_specs=(vmem,) * 2,
        compiler_params=limit,
    )(lags, bare)
    polar = pl.pallas_call(
        order_kernel,
        out_shape=plane,
        in_specs=[vmem],
        out_specs=hbm,
        scratch_shapes=in_order,
        compiler_params=limit,
        cost_estimate=pl.CostEstimate(flops=1000, bytes_accessed=1000, transcendentals=0),
    )(polar_sorted)
    parity = (lax.axis_index("tile") % 2).astype(jnp.int32).reshape(1)
    screened = polar_sorted
    chip_pairs = [(i, i ^ 1) for i in range(n_tile)]
    far_pairs = [(i, i + 1 if i % 2 else i - 1) for i in range(1, n_tile - 1)]
    for step in range(ITERS):
        last = step == ITERS - 1
        far = lax.ppermute(resid_b, "tile", far_pairs)
        chip = lax.ppermute(resid_b, "tile", chip_pairs)
        near, base = pl.pallas_call(
            lambda *refs, first=step == 0: near_kernel(first, *refs),
            out_shape=(plane, plane),
            in_specs=[smem] + [vmem] * 6,
            out_specs=(vmem,) * 2,
            compiler_params=limit,
        )(parity, resid_b, chip, polar_sorted, screened, bare, precond)
        out = pl.pallas_call(
            lambda *refs, last=last: step_kernel(last, *refs),
            out_shape=(plane,) if last else (plane, plane_b),
            in_specs=[smem] + [vmem] * 6,
            out_specs=(hbm,) if last else (vmem, vmem),
            scratch_shapes=in_order if last else [],
            compiler_params=limit,
        )(parity, near, base, far, polar_sorted, bare, precond)
        screened = out[0]
        resid_b = out[-1]
    return (polar, screened)


def solution(mesh):
    placed = (
        P(None, "energy", "tile"),
        P(None, "energy", "tile"),
        P("tile"),
        P(None, "tile", None),
    )
    return jax.shard_map(
        per_device,
        mesh=mesh,
        in_specs=placed,
        out_specs=(P("energy", "tile"), P("energy", "tile")),
        check_vma=False,
    )
```
